32 devices in a mesh: groups: 2 (over y), section: 2 (over core), tensor: 8 (over z, x).
Axes of the slice: x: 2, y: 2, z: 4, core: 2. Of those that a mesh axis runs over, the one named last changes fastest.
Arguments:
- hidden_rows: bfloat16 [2048, 8192], P(('groups', 'tensor')), parts along dimension 0, may hold values from -500 to 500, as said below
- fresh_rows: bfloat16 [16, 2, 8192], P(('groups', 'tensor')), parts along dimension 0, may hold values from -500 to 500, as said below
- owners: int32 [2048, 1], P(('groups', 'tensor')), parts along dimension 0, may hold values from 0 to 7; in each aligned block of 128 rows (0 to 127, 128 to 255, ...) at most 32 rows name the same one
- key_weight: bfloat16 [8192, 512], P('tensor', 'section'), may hold values from -0.0625 to 0.0625
- value_weight: bfloat16 [8192, 512], P('tensor', 'section'), may hold values from -0.0625 to 0.0625
- queries: bfloat16 [16, 2, 4096], P(('groups', 'tensor'), None, 'section'), parts along dimension 0, may hold values from -170 to 170, as said below
- out_weight: bfloat16 [4096, 8192], P('section', 'tensor'), may hold values from -0.09375 to 0.09375
Outputs:
- attended: bfloat16 [16, 2, 8192], P('groups', None, 'tensor'), parts along dimension 0
The draws below stay inside these ranges and needn't reach their ends.
There are 2 independent parts, one for each index of `groups`. The reference program is written for one: setup_inputs(seed, part) draws one part's arguments, and reference() takes and returns one part's arrays. A program takes and returns all parts, laid end to end along the dimension named above; an argument that names none is the same for every part. Nothing has to cross between parts.
Inputs may be any that keep to these rules, and one draw needn't show every extreme that they name: `owners`: in the rows of one device (aligned blocks of 128 rows) no owner is named by more than 32 rows, a bound that some block reaches; every owner is named by some row. `hidden_rows`: saved activations of the layer's input. `fresh_rows`: activations of the layer's input. `queries`: queries after the rotary embedding.
All inputs are finite; a program needn't handle non-finite values.
Results may differ from the reference program's by a relative error of at most 0.0055.
The reference program's roundings to bfloat16 on the way count: a program that leaves them out, or rounds other values in their place, can miss the bound.
Values may be sent and summed in bfloat16 or wider, within the bound.
A program may use at most 64 MiB of HBM per device.

```python
import math
import jax
import jax.numpy as jnp
import numpy as np
from jax import lax

D = 8192
DH = 128
KVH = 4
NEW = 2
ROWS_DEV = 128
HQ = 32
CAP = 32
REQ = 8
ROWS = 1024
N_TENSOR = 8


def rough_rows(key, row_count, salt):
    base_key = jax.random.fold_in(key, salt)
    row_key = jax.random.fold_in(key, salt + 1)
    channel_key = jax.random.fold_in(key, 11)
    base = jnp.clip(jax.random.normal(base_key, (row_count, D), jnp.float32), -5.0, 5.0)
    row_scale = jnp.exp(jax.random.uniform(row_key, (row_count, 1), jnp.float32, 0.0, 2.3))
    channel_scale = jnp.exp(jax.random.uniform(channel_key, (1, D), jnp.float32, 0.0, 2.3))
    return base * row_scale * channel_scale


def draw_hidden_rows(key, part):
    return rough_rows(key, ROWS, 21).astype(jnp.bfloat16)


def draw_fresh_rows(key, part):
    return rough_rows(key, REQ * NEW, 31).reshape(REQ, NEW, D).astype(jnp.bfloat16)


def draw_queries(key, part):
    base_key = jax.random.fold_in(key, 41)
    values = jnp.clip(2.0 * jax.random.normal(base_key, (REQ, NEW, HQ * DH), jnp.float32), -8.0, 8.0)
    return values.astype(jnp.bfloat16)


def shard_levels(rng, dims, split, smallest, high):
    factor_of, own = 1.0, jax.random.fold_in(rng, 6)
    for position, blocks in split:
        heights = jnp.exp(jax.random.uniform(jax.random.fold_in(own, position), (blocks,), jnp.float32, smallest / len(split), high / len(split)))
        factor_of = factor_of * jnp.repeat(heights, dims[position] // blocks).reshape([-1 if axis == position else 1 for axis in range(len(dims))])
    return factor_of


def deal_out(rng, own, number, rows, count, top, bound, lean):
    order = jax.random.permutation(rng, count)
    heavy_load, ordinary = load_shares(count, rows * top, bound, lean, True), load_shares(count, rows * top, bound, lean, False)
    places = jnp.arange(count)

    def named(sizes, rotation):
        used = int((sizes > 0).sum())
        fixed = max(1, used // 4)
        passed = fixed + (places - fixed + rotation * (used - fixed)) % max(1, count - fixed)
        return jnp.zeros((count,), jnp.int32).at[order[jnp.where(places < fixed, places, passed)]].set(jnp.asarray(sizes, jnp.int32))

    sizes = jnp.where(number % 4 == 0, named(heavy_load, number // 4), named(ordinary, number - number // 4 - 1))
    mixed = jax.random.permutation(jax.random.fold_in(own, 3), count)
    donor, taker = mixed[0:count // 2 * 2:2], mixed[1:count // 2 * 2:2]
    room = jnp.minimum(sizes[donor] - 1, bound - sizes[taker]) // 2
    room = jnp.where((donor == order[0]) | (taker == order[0]) | (sizes[taker] == 0), 0, jnp.maximum(room, 0))
    passed = jax.random.randint(jax.random.fold_in(own, 4), (count // 2,), 0, 1 << 20) % (room + 1)
    sizes = sizes.at[donor].add(-passed).at[taker].add(passed)
    items = jnp.searchsorted(jnp.cumsum(sizes), jnp.arange(rows * top), side="right").astype(jnp.int32)
    table = items.reshape(top, rows).T
    table = table[jax.random.permutation(jax.random.fold_in(own, 1), rows)]
    rotation = jax.random.randint(jax.random.fold_in(own, 2), (rows, 1), 0, top)
    return jnp.take_along_axis(table, (jnp.arange(top)[None, :] + rotation) % top, axis=1)


def load_shares(number_of, total, most, slope, full):
    weights = [(1 << 20) // math.isqrt(grade ** slope) + 1 for grade in range(1, number_of + 1)]
    largest = most if full else min(most, max(-(-total // number_of), total * weights[0] // sum(weights)))
    least = 1 if total - largest >= number_of - 1 else 0
    holding, rest = [largest] + [least] * (number_of - 1), total - largest - least * (number_of - 1)
    while rest > 0:
        free = [i for i in range(1, number_of) if holding[i] < largest] or [i for i in range(1, number_of) if holding[i] < most]
        whole, left = sum([weights[i] for i in free]), rest
        for i in free:
            extra = min(most - holding[i], max(1, left * weights[i] // whole), rest)
            holding[i] = holding[i] + extra
            rest = rest - extra
    return np.array(holding)


def scatter_about(rng, extent, width, limit, cuts=(), kind=jnp.bfloat16):
    factor_of = shard_levels(rng, extent, cuts, -0.22, 0.18) if cuts else 1.0
    result = jax.random.normal(rng, extent, jnp.float32) * width * factor_of
    return jnp.minimum(jnp.maximum(result, -limit), limit).astype(kind)


def setup_inputs(seed: int = 0, part: int = 0) -> dict:
    seeds = jax.random.split(jax.random.key(seed), 8)
    own_keys = jax.random.split(jax.random.fold_in(seeds[7], part), 8)
    hidden_rows = draw_hidden_rows(jax.random.fold_in(jax.random.fold_in(seeds[7], part), 71), part)
    fresh_rows = draw_fresh_rows(jax.random.fold_in(jax.random.fold_in(seeds[7], part), 71), part)
    owners_keys = jax.random.split(jax.random.fold_in(own_keys[2], 1), ROWS // ROWS_DEV)
    owners_turns = jax.random.permutation(jax.random.fold_in(own_keys[2], 3), ROWS // ROWS_DEV)
    owners = jax.vmap(lambda own, number: deal_out(jax.random.fold_in(own_keys[2], 2), own, number, ROWS_DEV, N_TENSOR, 1, CAP, 2))(owners_keys, owners_turns).reshape((ROWS, 1))
    key_weight = scatter_about(seeds[3], (D, KVH * DH), D ** -0.5, 0.0625, ((0, 8), (1, 2)))
    value_weight = scatter_about(seeds[4], (D, KVH * DH), D ** -0.5, 0.0625, ((0, 8), (1, 2)))
    queries = draw_queries(jax.random.fold_in(jax.random.fold_in(seeds[7], part), 71), part)
    out_weight = scatter_about(seeds[6], (HQ * DH, D), (HQ * DH) ** -0.5, 0.09375, ((0, 2), (1, 8)))
    return {"hidden_rows": hidden_rows, "fresh_rows": fresh_rows, "owners": owners, "key_weight": key_weight, "value_weight": value_weight, "queries": queries, "out_weight": out_weight}


norm_eps = 1e-05

def rms_rows(row_block):
    widened = row_block.astype(jnp.float32)
    factor = lax.rsqrt(lax.optimization_barrier(jnp.mean(widened * widened, axis=-1, keepdims=True)) + norm_eps)
    return (widened * factor).astype(jnp.bfloat16)

def attend(query_rows, cache_keys, cache_values, cache_valid, fresh_keys, fresh_values):
    steps_new = query_rows.shape[0]
    kv_heads = cache_keys.shape[1] // DH
    group_size = query_rows.shape[1] // (kv_heads * DH)
    query_heads = query_rows.astype(jnp.float32).reshape(steps_new, kv_heads, group_size, DH)
    cache_k = cache_keys.astype(jnp.float32).reshape(-1, kv_heads, DH)
    cache_v = cache_values.astype(jnp.float32).reshape(-1, kv_heads, DH)
    fresh_k = fresh_keys.astype(jnp.float32).reshape(-1, kv_heads, DH)
    fresh_v = fresh_values.astype(jnp.float32).reshape(-1, kv_heads, DH)
    cache_scores = jnp.einsum('tkgd,skd->tkgs', query_heads, cache_k) / math.sqrt(DH)
    fresh_scores = jnp.einsum('tkgd,skd->tkgs', query_heads, fresh_k) / math.sqrt(DH)
    visible = jnp.arange(steps_new)[None, :] <= jnp.arange(steps_new)[:, None]
    cache_mask = cache_valid[None, None, None, :]
    fresh_mask = visible[:, None, None, :]
    cache_scores = jnp.where(cache_mask, cache_scores, -1e+30)
    fresh_scores = jnp.where(fresh_mask, fresh_scores, -1e+30)
    highest = jnp.maximum(lax.optimization_barrier(jnp.max(cache_scores, axis=-1)), lax.optimization_barrier(jnp.max(fresh_scores, axis=-1)))[..., None]
    cache_weights = jnp.where(cache_mask, jnp.exp(cache_scores - highest), 0.0)
    fresh_weights = jnp.where(fresh_mask, jnp.exp(fresh_scores - highest), 0.0)
    weight_sum = lax.optimization_barrier(jnp.sum(cache_weights, axis=-1)) + lax.optimization_barrier(jnp.sum(fresh_weights, axis=-1))
    cache_round = cache_weights.astype(jnp.bfloat16).astype(jnp.float32)
    fresh_round = fresh_weights.astype(jnp.bfloat16).astype(jnp.float32)
    blended = jnp.einsum('tkgs,skd->tkgd', cache_round, cache_v) + jnp.einsum('tkgs,skd->tkgd', fresh_round, fresh_v)
    result_heads = blended / weight_sum[..., None]
    return result_heads.reshape(steps_new, -1).astype(jnp.bfloat16)

def reference(hidden_rows, fresh_rows, owners, key_weight, value_weight, queries, out_weight):
    normed = rms_rows(hidden_rows)
    cache_keys = jnp.dot(normed, key_weight, preferred_element_type=jnp.float32).astype(jnp.bfloat16)
    cache_values = jnp.dot(normed, value_weight, preferred_element_type=jnp.float32).astype(jnp.bfloat16)
    fresh_normed = rms_rows(fresh_rows.reshape(REQ * NEW, D))
    fresh_keys = jnp.dot(fresh_normed, key_weight, preferred_element_type=jnp.float32).astype(jnp.bfloat16)
    fresh_values = jnp.dot(fresh_normed, value_weight, preferred_element_type=jnp.float32).astype(jnp.bfloat16)
    fresh_keys = fresh_keys.reshape(REQ, NEW, KVH * DH)
    fresh_values = fresh_values.reshape(REQ, NEW, KVH * DH)
    owner_list = owners[:, 0]

    def one_request(request):
        return attend(queries[request], cache_keys, cache_values, owner_list == request, fresh_keys[request], fresh_values[request])
    head_outputs = lax.map(one_request, jnp.arange(REQ, dtype=jnp.int32))
    attended = jnp.dot(head_outputs.reshape(REQ * NEW, HQ * DH), out_weight, preferred_element_type=jnp.float32)
    return attended.astype(jnp.bfloat16).reshape(REQ, NEW, D)
```

```python
import functools
import math

import jax
import jax.numpy as jnp
from jax import lax
from jax.experimental import pallas as pl
from jax.experimental.pallas import tpu as pltpu
from jax.sharding import PartitionSpec as P

DH = 128


norm_eps = 1e-05


def rms_rows(row_block):
    widened = row_block.astype(jnp.float32)
    factor = lax.rsqrt(jnp.mean(widened * widened, axis=-1, keepdims=True) + norm_eps)
    return (widened * factor).astype(jnp.bfloat16)


def attend(query_rows, cache_keys, cache_values, cache_valid, fresh_keys, fresh_values):
    steps_new = query_rows.shape[0]
    kv_heads = cache_keys.shape[1] // DH
    group_size = query_rows.shape[1] // (kv_heads * DH)
    query_heads = query_rows.reshape(steps_new, kv_heads, group_size, DH)
    cache_k = cache_keys.reshape(-1, kv_heads, DH)
    cache_v = cache_values.reshape(-1, kv_heads, DH)
    fresh_k = fresh_keys.reshape(-1, kv_heads, DH)
    fresh_v = fresh_values.reshape(-1, kv_heads, DH)
    cache_scores = jnp.einsum(
        "tkgd,skd->tkgs", query_heads, cache_k, preferred_element_type=jnp.float32
    ) / math.sqrt(DH)
    fresh_scores = jnp.einsum(
        "tkgd,skd->tkgs", query_heads, fresh_k, preferred_element_type=jnp.float32
    ) / math.sqrt(DH)
    visible = jnp.arange(steps_new)[None, :] <= jnp.arange(steps_new)[:, None]
    cache_mask = cache_valid[None, None, None, :]
    fresh_mask = visible[:, None, None, :]
    cache_scores = jnp.where(cache_mask, cache_scores, -1e30)
    fresh_scores = jnp.where(fresh_mask, fresh_scores, -1e30)
    highest = jnp.maximum(jnp.max(cache_scores, axis=-1), jnp.max(fresh_scores, axis=-1))[..., None]
    cache_weights = jnp.where(cache_mask, jnp.exp(cache_scores - highest), 0.0)
    fresh_weights = jnp.where(fresh_mask, jnp.exp(fresh_scores - highest), 0.0)
    weight_sum = jnp.sum(cache_weights, axis=-1) + jnp.sum(fresh_weights, axis=-1)
    blended = jnp.einsum(
        "tkgs,skd->tkgd",
        cache_weights.astype(jnp.bfloat16),
        cache_v,
        preferred_element_type=jnp.float32,
    )
    blended = blended + jnp.einsum(
        "tkgs,skd->tkgd",
        fresh_weights.astype(jnp.bfloat16),
        fresh_v,
        preferred_element_type=jnp.float32,
    )
    result_heads = blended / weight_sum[..., None]
    return result_heads.reshape(steps_new, -1).astype(jnp.bfloat16)


def project_rows(normed, key_weight, value_weight):
    key_sums = jnp.dot(
        normed,
        lax.all_gather(key_weight, "tensor", axis=0, tiled=True),
        preferred_element_type=jnp.float32,
    )
    value_sums = jnp.dot(
        normed,
        lax.all_gather(value_weight, "tensor", axis=0, tiled=True),
        preferred_element_type=jnp.float32,
    )
    return (key_sums.astype(jnp.bfloat16), value_sums.astype(jnp.bfloat16))


def slot_layout(owners, peers, capacity):
    target = owners[:, 0]
    onehot = (target[:, None] == jnp.arange(peers, dtype=jnp.int32)[None, :]).astype(jnp.int32)
    rows = jnp.arange(target.shape[0], dtype=jnp.int32)
    earlier = (target[:, None] == target[None, :]) & (rows[None, :] < rows[:, None])
    within = jnp.sum(earlier.astype(jnp.int32), axis=1)
    counts = jnp.sum(onehot, axis=0)
    return (target * capacity + within, counts)


def fill_slots(payload, slot_index, peers, capacity):
    buffer = (
        jnp.zeros((peers * capacity, payload.shape[1]), payload.dtype).at[slot_index].set(payload)
    )
    return buffer.reshape(peers, capacity, payload.shape[1])


def gathered_weights(hidden_rows, fresh_rows, owners, key_weight, value_weight, queries, out_weight):
    peers = lax.axis_size("tensor")
    rows_here = hidden_rows.shape[0]
    capacity = max(2, 2 * rows_here // peers)
    slot_index, counts = slot_layout(owners, peers, capacity)
    slot_total = peers * capacity
    normed = rms_rows(jnp.concatenate([hidden_rows, fresh_rows[0]], axis=0))
    key_rows, value_rows = project_rows(normed, key_weight, value_weight)
    local_pairs = jnp.concatenate([key_rows[:rows_here], value_rows[:rows_here]], axis=1)
    outgoing = fill_slots(local_pairs, slot_index, peers, capacity)
    arrived, arrived_counts = (
        lax.all_to_all(outgoing, "tensor", split_axis=0, concat_axis=0, tiled=True),
        lax.all_to_all(counts.reshape(peers, 1), "tensor", split_axis=0, concat_axis=0, tiled=True),
    )
    flat_pairs = arrived.reshape(slot_total, -1)
    half_width = key_rows.shape[1]
    cache_keys, cache_values = (flat_pairs[:, :half_width], flat_pairs[:, half_width:])
    fresh_keys, fresh_values = (key_rows[rows_here:], value_rows[rows_here:])
    cache_valid = (jnp.arange(capacity, dtype=jnp.int32)[None, :] < arrived_counts).reshape(-1)
    head_block = attend(queries[0], cache_keys, cache_values, cache_valid, fresh_keys, fresh_values)
    piece = lax.all_gather(head_block[None], "tensor", axis=0, tiled=True)
    flat_piece = piece.reshape(-1, piece.shape[-1])
    partial_rows = jnp.dot(flat_piece, out_weight, preferred_element_type=jnp.float32)
    partial_out = partial_rows.reshape(piece.shape[0], piece.shape[1], -1)
    summed = lax.psum(partial_out, "section")
    return summed.astype(jnp.bfloat16)


def row_factor(widened_squares, width):
    return lax.rsqrt(widened_squares / width + norm_eps)


def weight_pieces(chunks, share):
    pieces = []
    for chunk in range(chunks):
        cuts = 1 if chunk == chunks - 1 else 1
        rows = share // cuts
        pieces.extend((chunk, cut * rows, rows) for cut in range(cuts))
    return pieces


def rebuild_kernel(
    peers,
    groups,
    hidden_hbm,
    fresh_hbm,
    owner_hbm,
    key_hbm,
    value_hbm,
    query_hbm,
    out_weight_hbm,
    out_ref,
    fresh_ref,
    owner_row,
    key_ref,
    value_ref,
    query_ref,
    own_rows,
    normed,
    fresh_normed,
    lhs,
    fresh_in,
    far_weights,
    parts,
    parts_x,
    parts_z,
    parts_in,
    outgoing,
    arrived,
    owner_all,
    queries_by_head,
    heads,
    heads_rounded,
    heads_all,
    heads_flat,
    out_weight,
    section_out,
    section_in,
    local_sem,
    weight_send,
    weight_recv,
    pass_send,
    pass_recv,
    act_send,
    act_recv,
    twin_send,
    twin_recv,
    fresh_send,
    fresh_recv,
    x_send,
    x_recv,
    z_send,
    z_recv,
    part_send,
    part_recv,
    owner_send,
    owner_recv,
    slot_send,
    slot_recv,
    head_send,
    head_recv,
    sec_send,
    sec_recv,
    met_sem,
):
    quad = peers // 2
    me = lax.axis_index("tensor")
    core = lax.axis_index("section")
    group = lax.axis_index("groups")
    q = lax.rem(me, quad)
    half = me // quad
    x_of = lax.rem(me, 2)
    z_of = q // 2

    def peer(relation):
        z = 1 - z_of if relation & 1 else z_of
        x = 1 - x_of if relation & 2 else x_of
        h = 1 - half if relation & 4 else half
        return h * quad + z * 2 + x

    def piece_of(relation):
        return peer(relation & 3) - half * quad

    rows_half = own_rows.shape[0]
    rows_here = 2 * rows_half
    width = own_rows.shape[1]
    piece = width // peers
    kv_width = key_ref.shape[1]
    share = piece // groups
    padded = lhs.shape[2]
    sent_rows = parts_in.shape[2]

    def remote(source, target, send, recv, **where):
        return pltpu.make_async_remote_copy(
            src_ref=source,
            dst_ref=target,
            send_sem=send,
            recv_sem=recv,
            device_id=where,
            device_id_type=pl.DeviceIdType.MESH,
        )

    rows_mine = pl.ds(pl.multiple_of(core * rows_half, rows_half), rows_half)
    load_rows = pltpu.make_async_copy(hidden_hbm.at[rows_mine, :], own_rows, local_sem.at[0])
    load_rows.start()
    load_owner = pltpu.make_async_copy(owner_hbm, owner_row, local_sem.at[1])
    load_fresh = pltpu.make_async_copy(fresh_hbm, fresh_ref, local_sem.at[2])
    load_key = pltpu.make_async_copy(key_hbm, key_ref, local_sem.at[3])
    load_value = pltpu.make_async_copy(value_hbm, value_ref, local_sem.at[4])
    load_query = pltpu.make_async_copy(query_hbm, query_ref, local_sem.at[5])
    load_out = pltpu.make_async_copy(out_weight_hbm, out_weight, local_sem.at[6])
    load_owner.start()
    load_fresh.start()
    load_key.start()
    load_value.start()

    far_first = (7, 5, 6, 4, 3, 1, 2)
    barrier = pltpu.get_barrier_semaphore()
    for relation in (5, 3, 1, 2):
        pl.semaphore_signal(
            barrier, inc=1, device_id={"tensor": peer(relation)},
            device_id_type=pl.DeviceIdType.MESH,
        )
    pl.semaphore_signal(
        barrier, inc=1, device_id={"groups": 1 - group}, device_id_type=pl.DeviceIdType.MESH
    )
    pl.semaphore_signal(
        barrier, inc=1, device_id={"section": 1 - core}, device_id_type=pl.DeviceIdType.MESH
    )

    chunks = 2 * kv_width // DH
    per_weight = kv_width // DH
    pieces = weight_pieces(chunks, share)
    weight_copies = []
    pass_refs = []
    for index, (chunk, first_row, rows) in enumerate(pieces):
        weight = (key_hbm, value_hbm)[chunk // per_weight]
        first = (chunk % per_weight) * DH
        span = pl.ds(pl.multiple_of(group * share + first_row, 16), rows)
        weight_copies.append(
            remote(
                weight.at[span, first : first + DH],
                far_weights.at[chunk, span, :],
                weight_send.at[index],
                weight_recv.at[index],
                tensor=peer(5),
            )
        )
        pass_refs.append(far_weights.at[chunk, span, :])

    load_rows.wait()
    squares = jnp.zeros((rows_half, 1), jnp.float32)
    for slice_index in range(peers):
        block = own_rows[:, slice_index * piece : (slice_index + 1) * piece].astype(jnp.float32)
        squares = squares + jnp.sum(block * block, axis=-1, keepdims=True)
    factor = row_factor(squares, width)
    for slice_index in range(peers):
        side = lax.rem(slice_index // quad + half, 2)
        block = own_rows[:, slice_index * piece : (slice_index + 1) * piece].astype(jnp.float32)
        normed[lax.rem(slice_index + 2 * side, quad), side] = (block * factor).astype(jnp.bfloat16)
    pl.semaphore_wait(barrier, 6)

    act_copies = {}
    twin_copies = {}

    def to_twin(source, relation):
        copy = remote(
            source,
            lhs.at[:, relation, rows_mine, :],
            twin_send.at[relation],
            twin_recv.at[relation],
            section=1 - core,
        )
        copy.start()
        twin_copies[relation] = copy

    for relation in (3, 1, 2):
        copy = remote(
            normed.at[piece_of(relation)],
            lhs.at[:, relation, rows_mine, :],
            act_send.at[relation],
            act_recv.at[relation],
            tensor=peer(relation),
        )
        copy.start()
        act_copies[relation] = copy
    to_twin(normed.at[q], 0)
    ahead = 3
    for copy in weight_copies[:ahead]:
        copy.start()
    pl.semaphore_signal(
        met_sem, inc=1, device_id={"tensor": peer(5)}, device_id_type=pl.DeviceIdType.MESH
    )
    load_query.start()
    load_out.start()
    lhs[:, 0, rows_mine, :] = normed[q]

    load_fresh.wait()
    fresh = fresh_ref[0].astype(jnp.float32)
    fresh_factor = row_factor(jnp.sum(fresh * fresh, axis=-1, keepdims=True), width)
    for slice_index in range(peers):
        side = lax.rem(slice_index // quad + half, 2)
        block = fresh[:, slice_index * piece : (slice_index + 1) * piece]
        fresh_normed[lax.rem(slice_index + 2 * side, quad), side] = block * fresh_factor
    fresh_copies = {}
    for relation in (3, 1, 2):
        copy = remote(
            fresh_normed.at[piece_of(relation)],
            fresh_in.at[relation],
            fresh_send.at[relation],
            fresh_recv.at[relation],
            tensor=peer(relation),
        )
        copy.start()
        fresh_copies[relation] = copy
    fresh_in[0] = fresh_normed[q]

    load_owner.wait()
    pl.semaphore_wait(met_sem, 1)
    owner_copies = {}
    for relation in far_first:
        copy = remote(
            owner_row,
            owner_all.at[me],
            owner_send.at[relation],
            owner_recv.at[relation],
            tensor=peer(relation),
        )
        copy.start()
        owner_copies[relation] = copy
    owner_all[me] = owner_row[...]

    new = fresh.shape[0]
    capacity = arrived.shape[2]
    slots = peers * capacity
    rows_of = owner_row[...]
    earlier = lax.broadcasted_iota(jnp.int32, (rows_here, rows_here), 0) < lax.broadcasted_iota(
        jnp.int32, (rows_here, rows_here), 1
    )
    rows_float = jnp.broadcast_to(rows_of.astype(jnp.float32), (rows_here, rows_here))
    same = jnp.logical_and(rows_float.T == rows_float, earlier)
    within = jnp.sum(jnp.where(same, 1.0, 0.0), axis=0, keepdims=True).astype(jnp.int32)
    slot_of = rows_of * capacity + within
    slot_pick = jnp.where(
        lax.broadcasted_iota(jnp.int32, (slots, rows_here), 0) == slot_of, 1.0, 0.0
    ).astype(jnp.bfloat16)

    load_query.wait()
    kv_heads = kv_width // DH
    group_size = query_ref.shape[2] // (kv_heads * DH)
    for head in range(kv_heads * group_size):
        queries_by_head[head // group_size, pl.ds((head % group_size) * new, new), :] = query_ref[
            0, :, head * DH : (head + 1) * DH
        ].astype(jnp.float32)

    load_key.wait()
    load_value.wait()

    def add_block(relation):
        for side in range(2):
            lhs[side, relation, rows_here:, :] = jnp.zeros(
                (padded - rows_here, piece), jnp.bfloat16
            )
            lhs[side, relation, rows_here : rows_here + new, :] = fresh_in[relation, side].astype(
                jnp.bfloat16
            )
        near = lhs[0, relation]
        for which, weight in enumerate((key_ref, value_ref)):
            product = jnp.dot(near, weight[...], preferred_element_type=jnp.float32)
            for column in range(per_weight):
                parts[which * per_weight + column, relation] = product[
                    :, column * DH : (column + 1) * DH
                ]

    pass_copies = []

    def pass_on(chunk):
        for index, (of_chunk, _, _) in enumerate(pieces):
            if of_chunk != chunk:
                continue
            weight_copies[index].wait_recv()
            if index + ahead < len(pieces):
                weight_copies[index + ahead].start()
            copy = remote(
                pass_refs[index],
                pass_refs[index],
                pass_send.at[index],
                pass_recv.at[index],
                groups=1 - group,
            )
            copy.start()
            pass_copies.append((chunk, copy))

    part_copies = {}
    x_copies = {}
    z_copies = {}
    slot_copies = {}
    fresh_rows = {}
    fresh_pad = padded - rows_here

    def multiply_far(chunk):
        for of_chunk, copy in pass_copies:
            if of_chunk == chunk:
                copy.wait_recv()
        product = jnp.dot(
            lhs[1].reshape(quad * padded, piece),
            far_weights[chunk],
            preferred_element_type=jnp.float32,
        )
        parts[chunk] = parts[chunk] + product.reshape(quad, padded, DH)

    def send_x(chunk):
        copy = remote(
            parts.at[chunk, pl.ds(2, 2), pl.ds(0, sent_rows), :],
            parts_x.at[chunk],
            x_send.at[chunk],
            x_recv.at[chunk],
            tensor=peer(2),
        )
        copy.start()
        x_copies[chunk] = copy

    def send_z(chunk):
        x_copies[chunk].wait_recv()
        parts[chunk, 1, :sent_rows] = parts[chunk, 1, :sent_rows] + parts_x[chunk, 1]
        copy = remote(
            parts.at[chunk, 1, pl.ds(0, sent_rows), :],
            parts_z.at[chunk],
            z_send.at[chunk],
            z_recv.at[chunk],
            tensor=peer(1),
        )
        copy.start()
        z_copies[chunk] = copy

    def send_direct(chunk):
        for relation in (3, 1, 2):
            copy = remote(
                parts.at[chunk, relation, pl.ds(0, sent_rows), :],
                parts_in.at[chunk, relation - 1],
                part_send.at[chunk, relation],
                part_recv.at[chunk, relation],
                tensor=peer(relation),
            )
            copy.start()
            part_copies[chunk, relation] = copy

    def gather_rows(chunk):
        total = parts[chunk, 0, :sent_rows]
        if chunk in x_copies:
            z_copies[chunk].wait_recv()
            total = total + parts_x[chunk, 0] + parts_z[chunk]
        else:
            for relation in (2, 1, 3):
                part_copies[chunk, relation].wait_recv()
                total = total + parts_in[chunk, relation - 1]
        placed = jnp.dot(
            slot_pick,
            total[:rows_here].astype(jnp.bfloat16),
            preferred_element_type=jnp.float32,
        ).astype(jnp.bfloat16)
        outgoing[chunk] = placed.reshape(peers, capacity, DH)
        fresh_rows[chunk] = jnp.concatenate(
            [
                total[rows_here:],
                jnp.zeros((fresh_pad - (sent_rows - rows_here), DH), jnp.float32),
            ],
            axis=0,
        ).astype(jnp.bfloat16)

    def send_slots(first, count):
        span = pl.ds(first, count)
        for relation in far_first:
            copy = remote(
                outgoing.at[span, peer(relation)],
                arrived.at[span, me],
                slot_send.at[first, relation],
                slot_recv.at[first, relation],
                tensor=peer(relation),
            )
            copy.start()
            slot_copies[first, relation] = copy
        arrived[span, me] = outgoing[span, me]

    def wait_slots(first):
        for relation in far_first[::-1]:
            slot_copies[first, relation].wait_recv()

    twin_copies[0].wait_recv()
    add_block(0)
    pass_on(0)
    for relation in (2, 1, 3):
        act_copies[relation].wait_recv()
        to_twin(lhs.at[:, relation, rows_mine, :], relation)
    pass_on(1)
    for relation in (2, 1, 3):
        twin_copies[relation].wait_recv()
        fresh_copies[relation].wait_recv()
        add_block(relation)
    for relation in far_first:
        owner_copies[relation].wait_recv()
    slot_mask = []
    for source in range(peers):
        count = jnp.sum(jnp.where(owner_all[source] == me, 1.0, 0.0), axis=-1, keepdims=True)
        place = lax.broadcasted_iota(jnp.int32, (capacity, DH), 0).astype(jnp.float32)
        slot_mask.append(jnp.where(place < count, 1.0, 0.0))
    slot_mask = jnp.concatenate(slot_mask, axis=0).T
    query_rows = new * group_size
    cache_mask = slot_mask[:query_rows] > 0.5
    step_of = lax.rem(lax.broadcasted_iota(jnp.int32, (query_rows, fresh_pad), 0), new)
    fresh_mask = lax.broadcasted_iota(jnp.int32, (query_rows, fresh_pad), 1) <= step_of

    multiply_far(0)
    send_direct(0)
    pass_on(2)
    multiply_far(1)
    send_direct(1)
    gather_rows(0)
    pass_on(3)
    multiply_far(2)
    send_direct(2)
    gather_rows(1)
    send_slots(0, per_weight)
    multiply_far(3)
    send_direct(3)
    gather_rows(2)
    send_slots(2, 1)
    gather_rows(3)
    send_slots(3, 1)

    scale = math.sqrt(DH)
    contract_last = (((1,), (1,)), ((), ()))

    def weigh(kv_head):
        query = queries_by_head[kv_head].astype(jnp.bfloat16)
        cache_k = arrived[kv_head].reshape(slots, DH)
        cache_scores = (
            lax.dot_general(query, cache_k, contract_last, preferred_element_type=jnp.float32)
            / scale
        )
        fresh_scores = (
            lax.dot_general(
                query, fresh_rows[kv_head], contract_last, preferred_element_type=jnp.float32
            )
            / scale
        )
        cache_scores = jnp.where(cache_mask, cache_scores, -1e30)
        fresh_scores = jnp.where(fresh_mask, fresh_scores, -1e30)
        highest = jnp.maximum(
            jnp.max(cache_scores, axis=-1, keepdims=True),
            jnp.max(fresh_scores, axis=-1, keepdims=True),
        )
        cache_weights = jnp.where(cache_mask, jnp.exp(cache_scores - highest), 0.0)
        fresh_weights = jnp.where(fresh_mask, jnp.exp(fresh_scores - highest), 0.0)
        weight_sum = jnp.sum(cache_weights, axis=-1, keepdims=True) + jnp.sum(
            fresh_weights, axis=-1, keepdims=True
        )
        return cache_weights.astype(jnp.bfloat16), fresh_weights.astype(jnp.bfloat16), weight_sum

    head_copies = {}

    def blend(kv_head, weights):
        cache_weights, fresh_weights, weight_sum = weights
        cache_v = arrived[per_weight + kv_head].reshape(slots, DH)
        blended = jnp.dot(cache_weights, cache_v, preferred_element_type=jnp.float32) + jnp.dot(
            fresh_weights, fresh_rows[per_weight + kv_head], preferred_element_type=jnp.float32
        )
        result = blended / weight_sum
        for member in range(group_size):
            heads[:, member * DH : (member + 1) * DH] = result[member * new : (member + 1) * new]
        heads_rounded[kv_head] = heads[...].astype(jnp.bfloat16)
        for relation in far_first:
            copy = remote(
                heads_rounded.at[kv_head],
                heads_all.at[kv_head, me],
                head_send.at[kv_head, relation],
                head_recv.at[kv_head, relation],
                tensor=peer(relation),
            )
            copy.start()
            head_copies[kv_head, relation] = copy
        heads_all[kv_head, me] = heads_rounded[kv_head]

    kv_out = group_size * DH

    def gathered_heads(kv_head):
        for relation in far_first[::-1]:
            head_copies[kv_head, relation].wait_recv()
        for source in range(peers):
            heads_flat[kv_head, source * new : (source + 1) * new, :] = heads_all[
                kv_head, source
            ].astype(jnp.float32)
        return heads_flat[kv_head].astype(jnp.bfloat16)

    wait_slots(0)
    weights_of = [weigh(kv_head) for kv_head in range(kv_heads)]
    wait_slots(2)
    blend(0, weights_of[0])
    wait_slots(3)
    blend(1, weights_of[1])

    load_out.wait()
    out_half = section_out.shape[2]
    flat = gathered_heads(0)
    for part in range(2):
        section_out[part] = jnp.dot(
            flat,
            out_weight[:kv_out, part * out_half : (part + 1) * out_half],
            preferred_element_type=jnp.float32,
        )
    flat = gathered_heads(1)
    section_copies = {}
    for part in range(2):
        section_out[part] = section_out[part] + jnp.dot(
            flat,
            out_weight[kv_out:, part * out_half : (part + 1) * out_half],
            preferred_element_type=jnp.float32,
        )
        copy = remote(
            section_out.at[part],
            section_in.at[part],
            sec_send.at[part],
            sec_recv.at[part],
            section=1 - core,
        )
        copy.start()
        section_copies[part] = copy
    for part in range(2):
        section_copies[part].wait_recv()
        out_ref[:, part * out_half : (part + 1) * out_half] = (
            section_out[part] + section_in[part]
        ).astype(jnp.bfloat16)

    for copies in (
        act_copies, twin_copies, fresh_copies, owner_copies, x_copies, z_copies, part_copies,
        slot_copies, head_copies, section_copies,
    ):
        for copy in copies.values():
            copy.wait_send()
    for copy in weight_copies:
        copy.wait_send()
    for _, copy in pass_copies:
        copy.wait_send()


def split_contraction(hidden_rows, fresh_rows, owners, key_weight, value_weight, queries, out_weight):
    peers = lax.axis_size("tensor")
    groups = lax.axis_size("groups")
    quad = peers // 2
    rows_here, width = hidden_rows.shape
    new = fresh_rows.shape[1]
    piece = width // peers
    kv_width = key_weight.shape[1]
    capacity = max(2, 2 * rows_here // peers)
    padded = rows_here + 16
    sent_rows = rows_here + 8
    query_width = queries.shape[2]
    kv_heads = kv_width // DH
    query_rows = new * query_width // (kv_heads * DH)
    out_width = out_weight.shape[1]
    bf16, f32 = jnp.bfloat16, jnp.float32
    dma = pltpu.SemaphoreType.DMA
    in_vmem = pl.BlockSpec(memory_space=pltpu.VMEM)
    in_hbm = pl.BlockSpec(memory_space=pltpu.HBM)
    chunks = 2 * kv_width // DH
    pieces = len(weight_pieces(chunks, piece // groups))
    flat = pl.pallas_call(
        functools.partial(rebuild_kernel, peers, groups),
        out_shape=jax.ShapeDtypeStruct((peers * new, out_width), bf16),
        in_specs=[in_hbm] * 7,
        out_specs=in_vmem,
        scratch_shapes=[
            pltpu.VMEM(fresh_rows.shape, bf16),
            pltpu.VMEM((1, rows_here), jnp.int32),
            pltpu.VMEM(key_weight.shape, bf16),
            pltpu.VMEM(value_weight.shape, bf16),
            pltpu.VMEM(queries.shape, bf16),
            pltpu.VMEM((rows_here // 2, width), bf16),
            pltpu.VMEM((quad, 2, rows_here // 2, piece), bf16),
            pltpu.VMEM((quad, 2, new, piece), f32),
            pltpu.VMEM((2, quad, padded, piece), bf16),
            pltpu.VMEM((quad, 2, new, piece), f32),
            pltpu.VMEM((chunks, piece, DH), bf16),
            pltpu.VMEM((chunks, quad, padded, DH), f32),
            pltpu.VMEM((chunks, 2, sent_rows, DH), f32),
            pltpu.VMEM((chunks, sent_rows, DH), f32),
            pltpu.VMEM((chunks, quad - 1, sent_rows, DH), f32),
            pltpu.VMEM((chunks, peers, capacity, DH), bf16),
            pltpu.VMEM((chunks, peers, capacity, DH), bf16),
            pltpu.VMEM((peers, 1, rows_here), jnp.int32),
            pltpu.VMEM((kv_heads, query_rows, DH), f32),
            pltpu.VMEM((new, query_width // kv_heads), f32),
            pltpu.VMEM((kv_heads, new, query_width // kv_heads), bf16),
            pltpu.VMEM((kv_heads, peers, new, query_width // kv_heads), bf16),
            pltpu.VMEM((kv_heads, peers * new, query_width // kv_heads), f32),
            pltpu.VMEM(out_weight.shape, bf16),
            pltpu.VMEM((2, peers * new, out_width // 2), f32),
            pltpu.VMEM((2, peers * new, out_width // 2), f32),
            dma((7,)),
            dma((pieces,)),
            dma((pieces,)),
            dma((pieces,)),
            dma((pieces,)),
            dma((quad,)),
            dma((quad,)),
            dma((quad,)),
            dma((quad,)),
            dma((quad,)),
            dma((quad,)),
            dma((chunks,)),
            dma((chunks,)),
            dma((chunks,)),
            dma((chunks,)),
            dma((chunks, quad)),
            dma((chunks, quad)),
            dma((peers,)),
            dma((peers,)),
            dma((chunks, peers)),
            dma((chunks, peers)),
            dma((kv_heads, peers)),
            dma((kv_heads, peers)),
            dma((2,)),
            dma((2,)),
            pltpu.SemaphoreType.REGULAR,
        ],
        compiler_params=pltpu.CompilerParams(
            collective_id=0, has_side_effects=True, vmem_limit_bytes=60 * 1024 * 1024
        ),
    )(
        hidden_rows,
        fresh_rows,
        owners.reshape(1, rows_here),
        key_weight,
        value_weight,
        queries,
        out_weight,
    )
    return flat.reshape(peers, new, out_width)


def per_device(hidden_rows, *others):
    peers = lax.axis_size("tensor")
    rows_here, width = hidden_rows.shape
    fits = (
        lax.axis_size("groups") == 2
        and lax.axis_size("section") == 2
        and peers == 8
        and width % (peers * 256) == 0
        and rows_here % 128 == 0
        and others[-1].shape[1] % 256 == 0
        and (2 * rows_here) % (peers * 16) == 0
    )
    if fits:
        return split_contraction(hidden_rows, *others)
    return gathered_weights(hidden_rows, *others)


def solution(mesh):
    return jax.shard_map(
        per_device,
        mesh=mesh,
        in_specs=(
            P(("groups", "tensor"), None),
            P(("groups", "tensor"), None, None),
            P(("groups", "tensor"), None),
            P("tensor", "section"),
            P("tensor", "section"),
            P(("groups", "tensor"), None, "section"),
            P("section", "tensor"),
        ),
        out_specs=P("groups", None, "tensor"),
        check_vma=False,
    )
```

```python
import functools
import math

import jax
import jax.numpy as jnp
from jax import lax
from jax.experimental import pallas as pl
from jax.experimental.pallas import tpu as pltpu
from jax.sharding import PartitionSpec as P

DH = 128


norm_eps = 1e-05


def rms_rows(row_block):
    widened = row_block.astype(jnp.float32)
    factor = lax.rsqrt(jnp.mean(widened * widened, axis=-1, keepdims=True) + norm_eps)
    return (widened * factor).astype(jnp.bfloat16)


def attend(query_rows, cache_keys, cache_values, cache_valid, fresh_keys, fresh_values):
    steps_new = query_rows.shape[0]
    kv_heads = cache_keys.shape[1] // DH
    group_size = query_rows.shape[1] // (kv_heads * DH)
    query_heads = query_rows.reshape(steps_new, kv_heads, group_size, DH)
    cache_k = cache_keys.reshape(-1, kv_heads, DH)
    cache_v = cache_values.reshape(-1, kv_heads, DH)
    fresh_k = fresh_keys.reshape(-1, kv_heads, DH)
    fresh_v = fresh_values.reshape(-1, kv_heads, DH)
    cache_scores = jnp.einsum(
        "tkgd,skd->tkgs", query_heads, cache_k, preferred_element_type=jnp.float32
    ) / math.sqrt(DH)
    fresh_scores = jnp.einsum(
        "tkgd,skd->tkgs", query_heads, fresh_k, preferred_element_type=jnp.float32
    ) / math.sqrt(DH)
    visible = jnp.arange(steps_new)[None, :] <= jnp.arange(steps_new)[:, None]
    cache_mask = cache_valid[None, None, None, :]
    fresh_mask = visible[:, None, None, :]
    cache_scores = jnp.where(cache_mask, cache_scores, -1e30)
    fresh_scores = jnp.where(fresh_mask, fresh_scores, -1e30)
    highest = jnp.maximum(jnp.max(cache_scores, axis=-1), jnp.max(fresh_scores, axis=-1))[..., None]
    cache_weights = jnp.where(cache_mask, jnp.exp(cache_scores - highest), 0.0)
    fresh_weights = jnp.where(fresh_mask, jnp.exp(fresh_scores - highest), 0.0)
    weight_sum = jnp.sum(cache_weights, axis=-1) + jnp.sum(fresh_weights, axis=-1)
    blended = jnp.einsum(
        "tkgs,skd->tkgd",
        cache_weights.astype(jnp.bfloat16),
        cache_v,
        preferred_element_type=jnp.float32,
    )
    blended = blended + jnp.einsum(
        "tkgs,skd->tkgd",
        fresh_weights.astype(jnp.bfloat16),
        fresh_v,
        preferred_element_type=jnp.float32,
    )
    result_heads = blended / weight_sum[..., None]
    return result_heads.reshape(steps_new, -1).astype(jnp.bfloat16)


def project_rows(normed, key_weight, value_weight):
    key_sums = jnp.dot(
        normed,
        lax.all_gather(key_weight, "tensor", axis=0, tiled=True),
        preferred_element_type=jnp.float32,
    )
    value_sums = jnp.dot(
        normed,
        lax.all_gather(value_weight, "tensor", axis=0, tiled=True),
        preferred_element_type=jnp.float32,
    )
    return (key_sums.astype(jnp.bfloat16), value_sums.astype(jnp.bfloat16))


def slot_layout(owners, peers, capacity):
    target = owners[:, 0]
    onehot = (target[:, None] == jnp.arange(peers, dtype=jnp.int32)[None, :]).astype(jnp.int32)
    rows = jnp.arange(target.shape[0], dtype=jnp.int32)
    earlier = (target[:, None] == target[None, :]) & (rows[None, :] < rows[:, None])
    within = jnp.sum(earlier.astype(jnp.int32), axis=1)
    counts = jnp.sum(onehot, axis=0)
    return (target * capacity + within, counts)


def fill_slots(payload, slot_index, peers, capacity):
    buffer = (
        jnp.zeros((peers * capacity, payload.shape[1]), payload.dtype).at[slot_index].set(payload)
    )
    return buffer.reshape(peers, capacity, payload.shape[1])


def gathered_weights(hidden_rows, fresh_rows, owners, key_weight, value_weight, queries, out_weight):
    peers = lax.axis_size("tensor")
    rows_here = hidden_rows.shape[0]
    capacity = max(2, 2 * rows_here // peers)
    slot_index, counts = slot_layout(owners, peers, capacity)
    slot_total = peers * capacity
    normed = rms_rows(jnp.concatenate([hidden_rows, fresh_rows[0]], axis=0))
    key_rows, value_rows = project_rows(normed, key_weight, value_weight)
    local_pairs = jnp.concatenate([key_rows[:rows_here], value_rows[:rows_here]], axis=1)
    outgoing = fill_slots(local_pairs, slot_index, peers, capacity)
    arrived, arrived_counts = (
        lax.all_to_all(outgoing, "tensor", split_axis=0, concat_axis=0, tiled=True),
        lax.all_to_all(counts.reshape(peers, 1), "tensor", split_axis=0, concat_axis=0, tiled=True),
    )
    flat_pairs = arrived.reshape(slot_total, -1)
    half_width = key_rows.shape[1]
    cache_keys, cache_values = (flat_pairs[:, :half_width], flat_pairs[:, half_width:])
    fresh_keys, fresh_values = (key_rows[rows_here:], value_rows[rows_here:])
    cache_valid = (jnp.arange(capacity, dtype=jnp.int32)[None, :] < arrived_counts).reshape(-1)
    head_block = attend(queries[0], cache_keys, cache_values, cache_valid, fresh_keys, fresh_values)
    piece = lax.all_gather(head_block[None], "tensor", axis=0, tiled=True)
    flat_piece = piece.reshape(-1, piece.shape[-1])
    partial_rows = jnp.dot(flat_piece, out_weight, preferred_element_type=jnp.float32)
    partial_out = partial_rows.reshape(piece.shape[0], piece.shape[1], -1)
    summed = lax.psum(partial_out, "section")
    return summed.astype(jnp.bfloat16)


def row_factor(widened_squares, width):
    return lax.rsqrt(widened_squares / width + norm_eps)


def weight_pieces(chunks, share):
    pieces = []
    for chunk in range(chunks):
        cuts = 2 if chunk == chunks - 1 else 1
        rows = share // cuts
        pieces.extend((chunk, cut * rows, rows) for cut in range(cuts))
    return pieces


def rebuild_kernel(
    peers,
    groups,
    hidden_hbm,
    fresh_hbm,
    owner_hbm,
    key_hbm,
    value_hbm,
    query_hbm,
    out_weight_hbm,
    out_ref,
    fresh_ref,
    owner_row,
    key_ref,
    value_ref,
    query_ref,
    own_rows,
    normed,
    fresh_normed,
    lhs,
    fresh_in,
    far_weights,
    parts,
    parts_x,
    parts_z,
    parts_in,
    outgoing,
    arrived,
    owner_all,
    queries_by_head,
    heads,
    heads_rounded,
    heads_all,
    heads_flat,
    out_weight,
    section_out,
    section_in,
    local_sem,
    weight_send,
    weight_recv,
    pass_send,
    pass_recv,
    act_send,
    act_recv,
    twin_send,
    twin_recv,
    fresh_send,
    fresh_recv,
    x_send,
    x_recv,
    z_send,
    z_recv,
    part_send,
    part_recv,
    owner_send,
    owner_recv,
    slot_send,
    slot_recv,
    head_send,
    head_recv,
    sec_send,
    sec_recv,
    met_sem,
):
    quad = peers // 2
    me = lax.axis_index("tensor")
    core = lax.axis_index("section")
    group = lax.axis_index("groups")
    q = lax.rem(me, quad)
    half = me // quad
    x_of = lax.rem(me, 2)
    z_of = q // 2

    def peer(relation):
        z = 1 - z_of if relation & 1 else z_of
        x = 1 - x_of if relation & 2 else x_of
        h = 1 - half if relation & 4 else half
        return h * quad + z * 2 + x

    def piece_of(relation):
        return peer(relation & 3) - half * quad

    rows_half = own_rows.shape[0]
    rows_here = 2 * rows_half
    width = own_rows.shape[1]
    piece = width // peers
    kv_width = key_ref.shape[1]
    share = piece // groups
    padded = lhs.shape[2]
    sent_rows = parts_in.shape[2]

    def remote(source, target, send, recv, **where):
        return pltpu.make_async_remote_copy(
            src_ref=source,
            dst_ref=target,
            send_sem=send,
            recv_sem=recv,
            device_id=where,
            device_id_type=pl.DeviceIdType.MESH,
        )

    rows_mine = pl.ds(pl.multiple_of(core * rows_half, rows_half), rows_half)
    load_rows = pltpu.make_async_copy(hidden_hbm.at[rows_mine, :], own_rows, local_sem.at[0])
    load_rows.start()
    load_owner = pltpu.make_async_copy(owner_hbm, owner_row, local_sem.at[1])
    load_fresh = pltpu.make_async_copy(fresh_hbm, fresh_ref, local_sem.at[2])
    load_key = pltpu.make_async_copy(key_hbm, key_ref, local_sem.at[3])
    load_value = pltpu.make_async_copy(value_hbm, value_ref, local_sem.at[4])
    load_query = pltpu.make_async_copy(query_hbm, query_ref, local_sem.at[5])
    load_out = pltpu.make_async_copy(out_weight_hbm, out_weight, local_sem.at[6])
    load_owner.start()
    load_fresh.start()
    load_key.start()
    load_value.start()

    far_first = (7, 5, 6, 4, 3, 1, 2)
    barrier = pltpu.get_barrier_semaphore()
    for relation in (5, 3, 1, 2):
        pl.semaphore_signal(
            barrier, inc=1, device_id={"tensor": peer(relation)},
            device_id_type=pl.DeviceIdType.MESH,
        )
    pl.semaphore_signal(
        barrier, inc=1, device_id={"groups": 1 - group}, device_id_type=pl.DeviceIdType.MESH
    )
    pl.semaphore_signal(
        barrier, inc=1, device_id={"section": 1 - core}, device_id_type=pl.DeviceIdType.MESH
    )

    chunks = 2 * kv_width // DH
    per_weight = kv_width // DH
    pieces = weight_pieces(chunks, share)
    weight_copies = []
    pass_refs = []
    for index, (chunk, first_row, rows) in enumerate(pieces):
        weight = (key_hbm, value_hbm)[chunk // per_weight]
        first = (chunk % per_weight) * DH
        span = pl.ds(pl.multiple_of(group * share + first_row, 16), rows)
        weight_copies.append(
            remote(
                weight.at[span, first : first + DH],
                far_weights.at[chunk, span, :],
                weight_send.at[index],
                weight_recv.at[index],
                tensor=peer(5),
            )
        )
        pass_refs.append(far_weights.at[chunk, span, :])

    load_rows.wait()
    squares = jnp.zeros((rows_half, 1), jnp.float32)
    for slice_index in range(peers):
        block = own_rows[:, slice_index * piece : (slice_index + 1) * piece].astype(jnp.float32)
        squares = squares + jnp.sum(block * block, axis=-1, keepdims=True)
    factor = row_factor(squares, width)
    for slice_index in range(peers):
        side = lax.rem(slice_index // quad + half, 2)
        block = own_rows[:, slice_index * piece : (slice_index + 1) * piece].astype(jnp.float32)
        normed[lax.rem(slice_index + 2 * side, quad), side] = (block * factor).astype(jnp.bfloat16)
    load_fresh.wait()
    fresh = fresh_ref[0].astype(jnp.float32)
    fresh_factor = row_factor(jnp.sum(fresh * fresh, axis=-1, keepdims=True), width)
    for slice_index in range(peers):
        side = lax.rem(slice_index // quad + half, 2)
        block = fresh[:, slice_index * piece : (slice_index + 1) * piece]
        fresh_normed[lax.rem(slice_index + 2 * side, quad), side] = block * fresh_factor
    pl.semaphore_wait(barrier, 6)

    act_copies = {}
    twin_copies = {}

    def to_twin(source, relation):
        copy = remote(
            source,
            lhs.at[:, relation, rows_mine, :],
            twin_send.at[relation],
            twin_recv.at[relation],
            section=1 - core,
        )
        copy.start()
        twin_copies[relation] = copy

    for relation in (3, 1, 2):
        copy = remote(
            normed.at[piece_of(relation)],
            lhs.at[:, relation, rows_mine, :],
            act_send.at[relation],
            act_recv.at[relation],
            tensor=peer(relation),
        )
        copy.start()
        act_copies[relation] = copy
    to_twin(normed.at[q], 0)
    fresh_copies = {}
    for relation in (3, 1, 2):
        copy = remote(
            fresh_normed.at[piece_of(relation)],
            fresh_in.at[relation],
            fresh_send.at[relation],
            fresh_recv.at[relation],
            tensor=peer(relation),
        )
        copy.start()
        fresh_copies[relation] = copy
    fresh_in[0] = fresh_normed[q]

    ahead = 99
    for copy in weight_copies[:ahead]:
        copy.start()
    pl.semaphore_signal(
        met_sem, inc=1, device_id={"tensor": peer(5)}, device_id_type=pl.DeviceIdType.MESH
    )
    load_query.start()
    load_out.start()
    lhs[:, 0, rows_mine, :] = normed[q]

    load_owner.wait()
    pl.semaphore_wait(met_sem, 1)
    owner_copies = {}
    for relation in far_first:
        copy = remote(
            owner_row,
            owner_all.at[me],
            owner_send.at[relation],
            owner_recv.at[relation],
            tensor=peer(relation),
        )
        copy.start()
        owner_copies[relation] = copy
    owner_all[me] = owner_row[...]

    new = fresh.shape[0]
    capacity = arrived.shape[2]
    slots = peers * capacity
    rows_of = owner_row[...]
    earlier = lax.broadcasted_iota(jnp.int32, (rows_here, rows_here), 0) < lax.broadcasted_iota(
        jnp.int32, (rows_here, rows_here), 1
    )
    rows_float = jnp.broadcast_to(rows_of.astype(jnp.float32), (rows_here, rows_here))
    same = jnp.logical_and(rows_float.T == rows_float, earlier)
    within = jnp.sum(jnp.where(same, 1.0, 0.0), axis=0, keepdims=True).astype(jnp.int32)
    slot_of = rows_of * capacity + within
    slot_pick = jnp.where(
        lax.broadcasted_iota(jnp.int32, (slots, rows_here), 0) == slot_of, 1.0, 0.0
    ).astype(jnp.bfloat16)

    load_query.wait()
    kv_heads = kv_width // DH
    group_size = query_ref.shape[2] // (kv_heads * DH)
    for head in range(kv_heads * group_size):
        queries_by_head[head // group_size, pl.ds((head % group_size) * new, new), :] = query_ref[
            0, :, head * DH : (head + 1) * DH
        ].astype(jnp.float32)

    load_key.wait()
    load_value.wait()

    def add_block(relation):
        for side in range(2):
            lhs[side, relation, rows_here:, :] = jnp.zeros(
                (padded - rows_here, piece), jnp.bfloat16
            )
            lhs[side, relation, rows_here : rows_here + new, :] = fresh_in[relation, side].astype(
                jnp.bfloat16
            )
        near = lhs[0, relation]
        for which, weight in enumerate((key_ref, value_ref)):
            product = jnp.dot(near, weight[...], preferred_element_type=jnp.float32)
            for column in range(per_weight):
                parts[which * per_weight + column, relation] = product[
                    :, column * DH : (column + 1) * DH
                ]

    pass_copies = []

    def pass_on(chunk):
        for index, (of_chunk, _, _) in enumerate(pieces):
            if of_chunk != chunk:
                continue
            weight_copies[index].wait_recv()
            copy = remote(
                pass_refs[index],
                pass_refs[index],
                pass_send.at[index],
                pass_recv.at[index],
                groups=1 - group,
            )
            copy.start()
            pass_copies.append((chunk, copy))

    part_copies = {}
    x_copies = {}
    z_copies = {}
    slot_copies = {}
    fresh_rows = {}
    fresh_pad = padded - rows_here

    def multiply_far(chunk):
        for of_chunk, copy in pass_copies:
            if of_chunk == chunk:
                copy.wait_recv()
        product = jnp.dot(
            lhs[1].reshape(quad * padded, piece),
            far_weights[chunk],
            preferred_element_type=jnp.float32,
        )
        parts[chunk] = parts[chunk] + product.reshape(quad, padded, DH)

    def send_x(chunk):
        copy = remote(
            parts.at[chunk, pl.ds(2, 2), pl.ds(0, sent_rows), :],
            parts_x.at[chunk],
            x_send.at[chunk],
            x_recv.at[chunk],
            tensor=peer(2),
        )
        copy.start()
        x_copies[chunk] = copy

    def send_z(chunk):
        x_copies[chunk].wait_recv()
        parts[chunk, 1, :sent_rows] = parts[chunk, 1, :sent_rows] + parts_x[chunk, 1]
        copy = remote(
            parts.at[chunk, 1, pl.ds(0, sent_rows), :],
            parts_z.at[chunk],
            z_send.at[chunk],
            z_recv.at[chunk],
            tensor=peer(1),
        )
        copy.start()
        z_copies[chunk] = copy

    def send_direct(chunk):
        for relation in (3, 1, 2):
            copy = remote(
                parts.at[chunk, relation, pl.ds(0, sent_rows), :],
                parts_in.at[chunk, relation - 1],
                part_send.at[chunk, relation],
                part_recv.at[chunk, relation],
                tensor=peer(relation),
            )
            copy.start()
            part_copies[chunk, relation] = copy

    def gather_rows(chunk):
        total = parts[chunk, 0, :sent_rows]
        if chunk in x_copies:
            z_copies[chunk].wait_recv()
            total = total + parts_x[chunk, 0] + parts_z[chunk]
        else:
            for relation in (2, 1, 3):
                part_copies[chunk, relation].wait_recv()
                total = total + parts_in[chunk, relation - 1]
        placed = jnp.dot(
            slot_pick,
            total[:rows_here].astype(jnp.bfloat16),
            preferred_element_type=jnp.float32,
        ).astype(jnp.bfloat16)
        outgoing[chunk] = placed.reshape(peers, capacity, DH)
        fresh_rows[chunk] = jnp.concatenate(
            [
                total[rows_here:],
                jnp.zeros((fresh_pad - (sent_rows - rows_here), DH), jnp.float32),
            ],
            axis=0,
        ).astype(jnp.bfloat16)

    def send_slots(first, count):
        span = pl.ds(first, count)
        for relation in far_first:
            copy = remote(
                outgoing.at[span, peer(relation)],
                arrived.at[span, me],
                slot_send.at[first, relation],
                slot_recv.at[first, relation],
                tensor=peer(relation),
            )
            copy.start()
            slot_copies[first, relation] = copy
        arrived[span, me] = outgoing[span, me]

    def wait_slots(first):
        for relation in far_first[::-1]:
            slot_copies[first, relation].wait_recv()

    twin_copies[0].wait_recv()
    add_block(0)
    for relation in (2, 1, 3):
        act_copies[relation].wait_recv()
        to_twin(lhs.at[:, relation, rows_mine, :], relation)
    for relation in (2, 1, 3):
        twin_copies[relation].wait_recv()
        fresh_copies[relation].wait_recv()
        add_block(relation)
    pass_on(0)
    pass_on(1)
    multiply_far(0)
    send_direct(0)
    pass_on(2)
    multiply_far(1)
    send_direct(1)
    pass_on(3)
    multiply_far(2)
    send_direct(2)
    multiply_far(3)
    send_direct(3)
    gather_rows(0)
    gather_rows(1)
    gather_rows(2)
    send_slots(0, per_weight)
    send_slots(2, 1)
    for relation in far_first:
        owner_copies[relation].wait_recv()
    slot_mask = []
    for source in range(peers):
        count = jnp.sum(jnp.where(owner_all[source] == me, 1.0, 0.0), axis=-1, keepdims=True)
        place = lax.broadcasted_iota(jnp.int32, (capacity, DH), 0).astype(jnp.float32)
        slot_mask.append(jnp.where(place < count, 1.0, 0.0))
    slot_mask = jnp.concatenate(slot_mask, axis=0).T
    query_rows = new * group_size
    cache_mask = slot_mask[:query_rows] > 0.5
    step_of = lax.rem(lax.broadcasted_iota(jnp.int32, (query_rows, fresh_pad), 0), new)
    fresh_mask = lax.broadcasted_iota(jnp.int32, (query_rows, fresh_pad), 1) <= step_of

    gather_rows(3)
    send_slots(3, 1)

    scale = math.sqrt(DH)
    contract_last = (((1,), (1,)), ((), ()))

    def weigh(kv_head):
        query = queries_by_head[kv_head].astype(jnp.bfloat16)
        cache_k = arrived[kv_head].reshape(slots, DH)
        cache_scores = (
            lax.dot_general(query, cache_k, contract_last, preferred_element_type=jnp.float32)
            / scale
        )
        fresh_scores = (
            lax.dot_general(
                query, fresh_rows[kv_head], contract_last, preferred_element_type=jnp.float32
            )
            / scale
        )
        cache_scores = jnp.where(cache_mask, cache_scores, -1e30)
        fresh_scores = jnp.where(fresh_mask, fresh_scores, -1e30)
        highest = jnp.maximum(
            jnp.max(cache_scores, axis=-1, keepdims=True),
            jnp.max(fresh_scores, axis=-1, keepdims=True),
        )
        cache_weights = jnp.where(cache_mask, jnp.exp(cache_scores - highest), 0.0)
        fresh_weights = jnp.where(fresh_mask, jnp.exp(fresh_scores - highest), 0.0)
        weight_sum = jnp.sum(cache_weights, axis=-1, keepdims=True) + jnp.sum(
            fresh_weights, axis=-1, keepdims=True
        )
        return cache_weights.astype(jnp.bfloat16), fresh_weights.astype(jnp.bfloat16), weight_sum

    head_copies = {}

    def blend(kv_head, weights):
        cache_weights, fresh_weights, weight_sum = weights
        cache_v = arrived[per_weight + kv_head].reshape(slots, DH)
        blended = jnp.dot(cache_weights, cache_v, preferred_element_type=jnp.float32) + jnp.dot(
            fresh_weights, fresh_rows[per_weight + kv_head], preferred_element_type=jnp.float32
        )
        result = blended / weight_sum
        for member in range(group_size):
            heads[:, member * DH : (member + 1) * DH] = result[member * new : (member + 1) * new]
        heads_rounded[kv_head] = heads[...].astype(jnp.bfloat16)
        for relation in far_first:
            copy = remote(
                heads_rounded.at[kv_head],
                heads_all.at[kv_head, me],
                head_send.at[kv_head, relation],
                head_recv.at[kv_head, relation],
                tensor=peer(relation),
            )
            copy.start()
            head_copies[kv_head, relation] = copy
        heads_all[kv_head, me] = heads_rounded[kv_head]

    kv_out = group_size * DH

    def gathered_heads(kv_head):
        for relation in far_first[::-1]:
            head_copies[kv_head, relation].wait_recv()
        for source in range(peers):
            heads_flat[kv_head, source * new : (source + 1) * new, :] = heads_all[
                kv_head, source
            ].astype(jnp.float32)
        return heads_flat[kv_head].astype(jnp.bfloat16)

    wait_slots(0)
    weights_of = [weigh(kv_head) for kv_head in range(kv_heads)]
    wait_slots(2)
    blend(0, weights_of[0])
    wait_slots(3)
    blend(1, weights_of[1])

    load_out.wait()
    out_half = section_out.shape[2]
    flat = gathered_heads(0)
    for part in range(2):
        section_out[part] = jnp.dot(
            flat,
            out_weight[:kv_out, part * out_half : (part + 1) * out_half],
            preferred_element_type=jnp.float32,
        )
    flat = gathered_heads(1)
    section_copies = {}
    for part in range(2):
        section_out[part] = section_out[part] + jnp.dot(
            flat,
            out_weight[kv_out:, part * out_half : (part + 1) * out_half],
            preferred_element_type=jnp.float32,
        )
        copy = remote(
            section_out.at[part],
            section_in.at[part],
            sec_send.at[part],
            sec_recv.at[part],
            section=1 - core,
        )
        copy.start()
        section_copies[part] = copy
    for part in range(2):
        section_copies[part].wait_recv()
        out_ref[:, part * out_half : (part + 1) * out_half] = (
            section_out[part] + section_in[part]
        ).astype(jnp.bfloat16)

    for copies in (
        act_copies, twin_copies, fresh_copies, owner_copies, x_copies, z_copies, part_copies,
        slot_copies, head_copies, section_copies,
    ):
        for copy in copies.values():
            copy.wait_send()
    for copy in weight_copies:
        copy.wait_send()
    for _, copy in pass_copies:
        copy.wait_send()


def split_contraction(hidden_rows, fresh_rows, owners, key_weight, value_weight, queries, out_weight):
    peers = lax.axis_size("tensor")
    groups = lax.axis_size("groups")
    quad = peers // 2
    rows_here, width = hidden_rows.shape
    new = fresh_rows.shape[1]
    piece = width // peers
    kv_width = key_weight.shape[1]
    capacity = max(2, 2 * rows_here // peers)
    padded = rows_here + 16
    sent_rows = rows_here + 8
    query_width = queries.shape[2]
    kv_heads = kv_width // DH
    query_rows = new * query_width // (kv_heads * DH)
    out_width = out_weight.shape[1]
    bf16, f32 = jnp.bfloat16, jnp.float32
    dma = pltpu.SemaphoreType.DMA
    in_vmem = pl.BlockSpec(memory_space=pltpu.VMEM)
    in_hbm = pl.BlockSpec(memory_space=pltpu.HBM)
    chunks = 2 * kv_width // DH
    pieces = len(weight_pieces(chunks, piece // groups))
    flat = pl.pallas_call(
        functools.partial(rebuild_kernel, peers, groups),
        out_shape=jax.ShapeDtypeStruct((peers * new, out_width), bf16),
        in_specs=[in_hbm] * 7,
        out_specs=in_vmem,
        scratch_shapes=[
            pltpu.VMEM(fresh_rows.shape, bf16),
            pltpu.VMEM((1, rows_here), jnp.int32),
            pltpu.VMEM(key_weight.shape, bf16),
            pltpu.VMEM(value_weight.shape, bf16),
            pltpu.VMEM(queries.shape, bf16),
            pltpu.VMEM((rows_here // 2, width), bf16),
            pltpu.VMEM((quad, 2, rows_here // 2, piece), bf16),
            pltpu.VMEM((quad, 2, new, piece), f32),
            pltpu.VMEM((2, quad, padded, piece), bf16),
            pltpu.VMEM((quad, 2, new, piece), f32),
            pltpu.VMEM((chunks, piece, DH), bf16),
            pltpu.VMEM((chunks, quad, padded, DH), f32),
            pltpu.VMEM((chunks, 2, sent_rows, DH), f32),
            pltpu.VMEM((chunks, sent_rows, DH), f32),
            pltpu.VMEM((chunks, quad - 1, sent_rows, DH), f32),
            pltpu.VMEM((chunks, peers, capacity, DH), bf16),
            pltpu.VMEM((chunks, peers, capacity, DH), bf16),
            pltpu.VMEM((peers, 1, rows_here), jnp.int32),
            pltpu.VMEM((kv_heads, query_rows, DH), f32),
            pltpu.VMEM((new, query_width // kv_heads), f32),
            pltpu.VMEM((kv_heads, new, query_width // kv_heads), bf16),
            pltpu.VMEM((kv_heads, peers, new, query_width // kv_heads), bf16),
            pltpu.VMEM((kv_heads, peers * new, query_width // kv_heads), f32),
            pltpu.VMEM(out_weight.shape, bf16),
            pltpu.VMEM((2, peers * new, out_width // 2), f32),
            pltpu.VMEM((2, peers * new, out_width // 2), f32),
            dma((7,)),
            dma((pieces,)),
            dma((pieces,)),
            dma((pieces,)),
            dma((pieces,)),
            dma((quad,)),
            dma((quad,)),
            dma((quad,)),
            dma((quad,)),
            dma((quad,)),
            dma((quad,)),
            dma((chunks,)),
            dma((chunks,)),
            dma((chunks,)),
            dma((chunks,)),
            dma((chunks, quad)),
            dma((chunks, quad)),
            dma((peers,)),
            dma((peers,)),
            dma((chunks, peers)),
            dma((chunks, peers)),
            dma((kv_heads, peers)),
            dma((kv_heads, peers)),
            dma((2,)),
            dma((2,)),
            pltpu.SemaphoreType.REGULAR,
        ],
        compiler_params=pltpu.CompilerParams(
            collective_id=0, has_side_effects=True, vmem_limit_bytes=60 * 1024 * 1024
        ),
    )(
        hidden_rows,
        fresh_rows,
        owners.reshape(1, rows_here),
        key_weight,
        value_weight,
        queries,
        out_weight,
    )
    return flat.reshape(peers, new, out_width)


def per_device(hidden_rows, *others):
    peers = lax.axis_size("tensor")
    rows_here, width = hidden_rows.shape
    fits = (
        lax.axis_size("groups") == 2
        and lax.axis_size("section") == 2
        and peers == 8
        and width % (peers * 256) == 0
        and rows_here % 128 == 0
        and others[-1].shape[1] % 256 == 0
        and (2 * rows_here) % (peers * 16) == 0
    )
    if fits:
        return split_contraction(hidden_rows, *others)
    return gathered_weights(hidden_rows, *others)


def solution(mesh):
    return jax.shard_map(
        per_device,
        mesh=mesh,
        in_specs=(
            P(("groups", "tensor"), None),
            P(("groups", "tensor"), None, None),
            P(("groups", "tensor"), None),
            P("tensor", "section"),
            P("tensor", "section"),
            P(("groups", "tensor"), None, "section"),
            P("section", "tensor"),
        ),
        out_specs=P("groups", None, "tensor"),
        check_vma=False,
    )
```

```python
import functools
import math

import jax
import jax.numpy as jnp
from jax import lax
from jax.experimental import pallas as pl
from jax.experimental.pallas import tpu as pltpu
from jax.sharding import PartitionSpec as P

DH = 128


norm_eps = 1e-05


def rms_rows(row_block):
    widened = row_block.astype(jnp.float32)
    factor = lax.rsqrt(jnp.mean(widened * widened, axis=-1, keepdims=True) + norm_eps)
    return (widened * factor).astype(jnp.bfloat16)


def attend(query_rows, cache_keys, cache_values, cache_valid, fresh_keys, fresh_values):
    steps_new = query_rows.shape[0]
    kv_heads = cache_keys.shape[1] // DH
    group_size = query_rows.shape[1] // (kv_heads * DH)
    query_heads = query_rows.reshape(steps_new, kv_heads, group_size, DH)
    cache_k = cache_keys.reshape(-1, kv_heads, DH)
    cache_v = cache_values.reshape(-1, kv_heads, DH)
    fresh_k = fresh_keys.reshape(-1, kv_heads, DH)
    fresh_v = fresh_values.reshape(-1, kv_heads, DH)
    cache_scores = jnp.einsum(
        "tkgd,skd->tkgs", query_heads, cache_k, preferred_element_type=jnp.float32
    ) / math.sqrt(DH)
    fresh_scores = jnp.einsum(
        "tkgd,skd->tkgs", query_heads, fresh_k, preferred_element_type=jnp.float32
    ) / math.sqrt(DH)
    visible = jnp.arange(steps_new)[None, :] <= jnp.arange(steps_new)[:, None]
    cache_mask = cache_valid[None, None, None, :]
    fresh_mask = visible[:, None, None, :]
    cache_scores = jnp.where(cache_mask, cache_scores, -1e30)
    fresh_scores = jnp.where(fresh_mask, fresh_scores, -1e30)
    highest = jnp.maximum(jnp.max(cache_scores, axis=-1), jnp.max(fresh_scores, axis=-1))[..., None]
    cache_weights = jnp.where(cache_mask, jnp.exp(cache_scores - highest), 0.0)
    fresh_weights = jnp.where(fresh_mask, jnp.exp(fresh_scores - highest), 0.0)
    weight_sum = jnp.sum(cache_weights, axis=-1) + jnp.sum(fresh_weights, axis=-1)
    blended = jnp.einsum(
        "tkgs,skd->tkgd",
        cache_weights.astype(jnp.bfloat16),
        cache_v,
        preferred_element_type=jnp.float32,
    )
    blended = blended + jnp.einsum(
        "tkgs,skd->tkgd",
        fresh_weights.astype(jnp.bfloat16),
        fresh_v,
        preferred_element_type=jnp.float32,
    )
    result_heads = blended / weight_sum[..., None]
    return result_heads.reshape(steps_new, -1).astype(jnp.bfloat16)


def project_rows(normed, key_weight, value_weight):
    key_sums = jnp.dot(
        normed,
        lax.all_gather(key_weight, "tensor", axis=0, tiled=True),
        preferred_element_type=jnp.float32,
    )
    value_sums = jnp.dot(
        normed,
        lax.all_gather(value_weight, "tensor", axis=0, tiled=True),
        preferred_element_type=jnp.float32,
    )
    return (key_sums.astype(jnp.bfloat16), value_sums.astype(jnp.bfloat16))


def slot_layout(owners, peers, capacity):
    target = owners[:, 0]
    onehot = (target[:, None] == jnp.arange(peers, dtype=jnp.int32)[None, :]).astype(jnp.int32)
    rows = jnp.arange(target.shape[0], dtype=jnp.int32)
    earlier = (target[:, None] == target[None, :]) & (rows[None, :] < rows[:, None])
    within = jnp.sum(earlier.astype(jnp.int32), axis=1)
    counts = jnp.sum(onehot, axis=0)
    return (target * capacity + within, counts)


def fill_slots(payload, slot_index, peers, capacity):
    buffer = (
        jnp.zeros((peers * capacity, payload.shape[1]), payload.dtype).at[slot_index].set(payload)
    )
    return buffer.reshape(peers, capacity, payload.shape[1])


def gathered_weights(hidden_rows, fresh_rows, owners, key_weight, value_weight, queries, out_weight):
    peers = lax.axis_size("tensor")
    rows_here = hidden_rows.shape[0]
    capacity = max(2, 2 * rows_here // peers)
    slot_index, counts = slot_layout(owners, peers, capacity)
    slot_total = peers * capacity
    normed = rms_rows(jnp.concatenate([hidden_rows, fresh_rows[0]], axis=0))
    key_rows, value_rows = project_rows(normed, key_weight, value_weight)
    local_pairs = jnp.concatenate([key_rows[:rows_here], value_rows[:rows_here]], axis=1)
    outgoing = fill_slots(local_pairs, slot_index, peers, capacity)
    arrived, arrived_counts = (
        lax.all_to_all(outgoing, "tensor", split_axis=0, concat_axis=0, tiled=True),
        lax.all_to_all(counts.reshape(peers, 1), "tensor", split_axis=0, concat_axis=0, tiled=True),
    )
    flat_pairs = arrived.reshape(slot_total, -1)
    half_width = key_rows.shape[1]
    cache_keys, cache_values = (flat_pairs[:, :half_width], flat_pairs[:, half_width:])
    fresh_keys, fresh_values = (key_rows[rows_here:], value_rows[rows_here:])
    cache_valid = (jnp.arange(capacity, dtype=jnp.int32)[None, :] < arrived_counts).reshape(-1)
    head_block = attend(queries[0], cache_keys, cache_values, cache_valid, fresh_keys, fresh_values)
    piece = lax.all_gather(head_block[None], "tensor", axis=0, tiled=True)
    flat_piece = piece.reshape(-1, piece.shape[-1])
    partial_rows = jnp.dot(flat_piece, out_weight, preferred_element_type=jnp.float32)
    partial_out = partial_rows.reshape(piece.shape[0], piece.shape[1], -1)
    summed = lax.psum(partial_out, "section")
    return summed.astype(jnp.bfloat16)


def row_factor(widened_squares, width):
    return lax.rsqrt(widened_squares / width + norm_eps)


def weight_pieces(chunks, share):
    pieces = []
    for chunk in range(chunks):
        cuts = 2 if chunk == chunks - 1 else 1
        rows = share // cuts
        pieces.extend((chunk, cut * rows, rows) for cut in range(cuts))
    return pieces


def rebuild_kernel(
    peers,
    groups,
    hidden_hbm,
    fresh_hbm,
    owner_hbm,
    key_hbm,
    value_hbm,
    query_hbm,
    out_weight_hbm,
    out_ref,
    fresh_ref,
    owner_row,
    key_ref,
    value_ref,
    query_ref,
    own_rows,
    normed,
    fresh_normed,
    lhs,
    fresh_in,
    far_weights,
    parts,
    parts_x,
    parts_z,
    parts_in,
    outgoing,
    arrived,
    owner_all,
    queries_by_head,
    heads,
    heads_rounded,
    heads_all,
    heads_flat,
    out_weight,
    section_out,
    section_in,
    local_sem,
    weight_send,
    weight_recv,
    pass_send,
    pass_recv,
    act_send,
    act_recv,
    twin_send,
    twin_recv,
    fresh_send,
    fresh_recv,
    x_send,
    x_recv,
    z_send,
    z_recv,
    part_send,
    part_recv,
    owner_send,
    owner_recv,
    slot_send,
    slot_recv,
    head_send,
    head_recv,
    sec_send,
    sec_recv,
    met_sem,
):
    quad = peers // 2
    me = lax.axis_index("tensor")
    core = lax.axis_index("section")
    group = lax.axis_index("groups")
    q = lax.rem(me, quad)
    half = me // quad
    x_of = lax.rem(me, 2)
    z_of = q // 2

    def peer(relation):
        z = 1 - z_of if relation & 1 else z_of
        x = 1 - x_of if relation & 2 else x_of
        h = 1 - half if relation & 4 else half
        return h * quad + z * 2 + x

    def piece_of(relation):
        return peer(relation & 3) - half * quad

    rows_half = own_rows.shape[0]
    rows_here = 2 * rows_half
    width = own_rows.shape[1]
    piece = width // peers
    kv_width = key_ref.shape[1]
    share = piece // groups
    padded = lhs.shape[2]
    sent_rows = parts_in.shape[2]

    def remote(source, target, send, recv, **where):
        return pltpu.make_async_remote_copy(
            src_ref=source,
            dst_ref=target,
            send_sem=send,
            recv_sem=recv,
            device_id=where,
            device_id_type=pl.DeviceIdType.MESH,
        )

    rows_mine = pl.ds(pl.multiple_of(core * rows_half, rows_half), rows_half)
    load_rows = pltpu.make_async_copy(hidden_hbm.at[rows_mine, :], own_rows, local_sem.at[0])
    load_rows.start()
    load_owner = pltpu.make_async_copy(owner_hbm, owner_row, local_sem.at[1])
    load_fresh = pltpu.make_async_copy(fresh_hbm, fresh_ref, local_sem.at[2])
    load_key = pltpu.make_async_copy(key_hbm, key_ref, local_sem.at[3])
    load_value = pltpu.make_async_copy(value_hbm, value_ref, local_sem.at[4])
    load_query = pltpu.make_async_copy(query_hbm, query_ref, local_sem.at[5])
    load_out = pltpu.make_async_copy(out_weight_hbm, out_weight, local_sem.at[6])
    load_owner.start()
    load_fresh.start()
    load_key.start()
    load_value.start()

    far_first = (7, 5, 6, 4, 3, 1, 2)
    barrier = pltpu.get_barrier_semaphore()
    for relation in (5, 3, 1, 2):
        pl.semaphore_signal(
            barrier, inc=1, device_id={"tensor": peer(relation)},
            device_id_type=pl.DeviceIdType.MESH,
        )
    pl.semaphore_signal(
        barrier, inc=1, device_id={"groups": 1 - group}, device_id_type=pl.DeviceIdType.MESH
    )
    pl.semaphore_signal(
        barrier, inc=1, device_id={"section": 1 - core}, device_id_type=pl.DeviceIdType.MESH
    )

    chunks = 2 * kv_width // DH
    per_weight = kv_width // DH
    pieces = weight_pieces(chunks, share)
    weight_copies = []
    pass_refs = []
    for index, (chunk, first_row, rows) in enumerate(pieces):
        weight = (key_hbm, value_hbm)[chunk // per_weight]
        first = (chunk % per_weight) * DH
        span = pl.ds(pl.multiple_of(group * share + first_row, 16), rows)
        weight_copies.append(
            remote(
                weight.at[span, first : first + DH],
                far_weights.at[chunk, span, :],
                weight_send.at[index],
                weight_recv.at[index],
                tensor=peer(5),
            )
        )
        pass_refs.append(far_weights.at[chunk, span, :])

    load_rows.wait()
    squares = jnp.zeros((rows_half, 1), jnp.float32)
    for slice_index in range(peers):
        block = own_rows[:, slice_index * piece : (slice_index + 1) * piece].astype(jnp.float32)
        squares = squares + jnp.sum(block * block, axis=-1, keepdims=True)
    factor = row_factor(squares, width)
    for slice_index in range(peers):
        side = lax.rem(slice_index // quad + half, 2)
        block = own_rows[:, slice_index * piece : (slice_index + 1) * piece].astype(jnp.float32)
        normed[lax.rem(slice_index + 2 * side, quad), side] = (block * factor).astype(jnp.bfloat16)
    load_fresh.wait()
    fresh = fresh_ref[0].astype(jnp.float32)
    fresh_factor = row_factor(jnp.sum(fresh * fresh, axis=-1, keepdims=True), width)
    for slice_index in range(peers):
        side = lax.rem(slice_index // quad + half, 2)
        block = fresh[:, slice_index * piece : (slice_index + 1) * piece]
        fresh_normed[lax.rem(slice_index + 2 * side, quad), side] = (block * fresh_factor).astype(
            jnp.bfloat16
        )
    pl.semaphore_wait(barrier, 6)

    act_copies = {}
    twin_copies = {}

    def to_twin(source, relation):
        copy = remote(
            source,
            lhs.at[:, relation, rows_mine, :],
            twin_send.at[relation],
            twin_recv.at[relation],
            section=1 - core,
        )
        copy.start()
        twin_copies[relation] = copy

    for relation in (3, 1, 2):
        copy = remote(
            normed.at[piece_of(relation)],
            lhs.at[:, relation, rows_mine, :],
            act_send.at[relation],
            act_recv.at[relation],
            tensor=peer(relation),
        )
        copy.start()
        act_copies[relation] = copy
    to_twin(normed.at[q], 0)
    fresh_copies = {}
    for relation in (3, 1, 2):
        copy = remote(
            fresh_normed.at[piece_of(relation)],
            fresh_in.at[relation],
            fresh_send.at[relation],
            fresh_recv.at[relation],
            tensor=peer(relation),
        )
        copy.start()
        fresh_copies[relation] = copy
    fresh_in[0] = fresh_normed[q]

    ahead = 99
    for copy in weight_copies[:ahead]:
        copy.start()
    pl.semaphore_signal(
        met_sem, inc=1, device_id={"tensor": peer(5)}, device_id_type=pl.DeviceIdType.MESH
    )
    load_query.start()
    load_out.start()
    lhs[:, 0, rows_mine, :] = normed[q]

    load_owner.wait()
    pl.semaphore_wait(met_sem, 1)
    owner_copies = {}
    for relation in far_first:
        copy = remote(
            owner_row,
            owner_all.at[me],
            owner_send.at[relation],
            owner_recv.at[relation],
            tensor=peer(relation),
        )
        copy.start()
        owner_copies[relation] = copy
    owner_all[me] = owner_row[...]

    new = fresh.shape[0]
    capacity = arrived.shape[2]
    slots = peers * capacity
    rows_of = owner_row[...]
    earlier = lax.broadcasted_iota(jnp.int32, (rows_here, rows_here), 0) < lax.broadcasted_iota(
        jnp.int32, (rows_here, rows_here), 1
    )
    rows_float = jnp.broadcast_to(rows_of.astype(jnp.float32), (rows_here, rows_here))
    same = jnp.logical_and(rows_float.T == rows_float, earlier)
    within = jnp.sum(jnp.where(same, 1.0, 0.0), axis=0, keepdims=True).astype(jnp.int32)
    slot_of = rows_of * capacity + within
    slot_pick = jnp.where(
        lax.broadcasted_iota(jnp.int32, (slots, rows_here), 0) == slot_of, 1.0, 0.0
    ).astype(jnp.bfloat16)

    load_query.wait()
    kv_heads = kv_width // DH
    group_size = query_ref.shape[2] // (kv_heads * DH)
    for head in range(kv_heads * group_size):
        queries_by_head[head // group_size, pl.ds((head % group_size) * new, new), :] = query_ref[
            0, :, head * DH : (head + 1) * DH
        ].astype(jnp.float32)

    load_key.wait()
    load_value.wait()

    def add_block(relation):
        for side in range(2):
            lhs[side, relation, rows_here:, :] = jnp.zeros(
                (padded - rows_here, piece), jnp.bfloat16
            )
            lhs[side, relation, rows_here : rows_here + new, :] = fresh_in[relation, side]
        near = lhs[0, relation]
        for which, weight in enumerate((key_ref, value_ref)):
            product = jnp.dot(near, weight[...], preferred_element_type=jnp.float32)
            for column in range(per_weight):
                parts[which * per_weight + column, relation] = product[
                    :, column * DH : (column + 1) * DH
                ]

    pass_copies = []

    def pass_on(chunk):
        for index, (of_chunk, _, _) in enumerate(pieces):
            if of_chunk != chunk:
                continue
            weight_copies[index].wait_recv()
            copy = remote(
                pass_refs[index],
                pass_refs[index],
                pass_send.at[index],
                pass_recv.at[index],
                groups=1 - group,
            )
            copy.start()
            pass_copies.append((chunk, copy))

    part_copies = {}
    x_copies = {}
    z_copies = {}
    slot_copies = {}
    fresh_rows = {}
    fresh_pad = padded - rows_here

    def multiply_far(chunk):
        for of_chunk, copy in pass_copies:
            if of_chunk == chunk:
                copy.wait_recv()
        product = jnp.dot(
            lhs[1].reshape(quad * padded, piece),
            far_weights[chunk],
            preferred_element_type=jnp.float32,
        )
        parts[chunk] = parts[chunk] + product.reshape(quad, padded, DH)

    def send_x(chunk):
        copy = remote(
            parts.at[chunk, pl.ds(2, 2), pl.ds(0, sent_rows), :],
            parts_x.at[chunk],
            x_send.at[chunk],
            x_recv.at[chunk],
            tensor=peer(2),
        )
        copy.start()
        x_copies[chunk] = copy

    def send_z(chunk):
        x_copies[chunk].wait_recv()
        parts[chunk, 1, :sent_rows] = parts[chunk, 1, :sent_rows] + parts_x[chunk, 1]
        copy = remote(
            parts.at[chunk, 1, pl.ds(0, sent_rows), :],
            parts_z.at[chunk],
            z_send.at[chunk],
            z_recv.at[chunk],
            tensor=peer(1),
        )
        copy.start()
        z_copies[chunk] = copy

    def send_direct(chunk):
        for relation in (2, 3, 1):
            copy = remote(
                parts.at[chunk, relation, pl.ds(0, sent_rows), :],
                parts_in.at[chunk, relation - 1],
                part_send.at[chunk, relation],
                part_recv.at[chunk, relation],
                tensor=peer(relation),
            )
            copy.start()
            part_copies[chunk, relation] = copy

    def gather_rows(chunk):
        total = parts[chunk, 0, :sent_rows]
        if chunk in x_copies:
            z_copies[chunk].wait_recv()
            total = total + parts_x[chunk, 0] + parts_z[chunk]
        else:
            for relation in (2, 1, 3):
                part_copies[chunk, relation].wait_recv()
                total = total + parts_in[chunk, relation - 1]
        placed = jnp.dot(
            slot_pick,
            total[:rows_here].astype(jnp.bfloat16),
            preferred_element_type=jnp.float32,
        ).astype(jnp.bfloat16)
        outgoing[chunk] = placed.reshape(peers, capacity, DH)
        fresh_rows[chunk] = jnp.concatenate(
            [
                total[rows_here:],
                jnp.zeros((fresh_pad - (sent_rows - rows_here), DH), jnp.float32),
            ],
            axis=0,
        ).astype(jnp.bfloat16)

    def send_slots(first, count):
        span = pl.ds(first, count)
        for relation in far_first:
            copy = remote(
                outgoing.at[span, peer(relation)],
                arrived.at[span, me],
                slot_send.at[first, relation],
                slot_recv.at[first, relation],
                tensor=peer(relation),
            )
            copy.start()
            slot_copies[first, relation] = copy
        arrived[span, me] = outgoing[span, me]

    def wait_slots(first):
        for relation in far_first[::-1]:
            slot_copies[first, relation].wait_recv()

    twin_copies[0].wait_recv()
    add_block(0)
    for relation in (3, 1, 2):
        act_copies[relation].wait_recv()
        to_twin(lhs.at[:, relation, rows_mine, :], relation)
    for relation in (3, 1, 2):
        twin_copies[relation].wait_recv()
        fresh_copies[relation].wait_recv()
        add_block(relation)
    pass_on(0)
    pass_on(1)
    multiply_far(0)
    send_direct(0)
    pass_on(2)
    multiply_far(1)
    send_direct(1)
    pass_on(3)
    multiply_far(2)
    send_direct(2)
    multiply_far(3)
    send_direct(3)
    gather_rows(0)
    gather_rows(1)
    gather_rows(2)
    send_slots(0, per_weight)
    send_slots(2, 1)
    for relation in far_first:
        owner_copies[relation].wait_recv()
    slot_mask = []
    for source in range(peers):
        count = jnp.sum(jnp.where(owner_all[source] == me, 1.0, 0.0), axis=-1, keepdims=True)
        place = lax.broadcasted_iota(jnp.int32, (capacity, DH), 0).astype(jnp.float32)
        slot_mask.append(jnp.where(place < count, 1.0, 0.0))
    slot_mask = jnp.concatenate(slot_mask, axis=0).T
    query_rows = new * group_size
    cache_mask = slot_mask[:query_rows] > 0.5
    step_of = lax.rem(lax.broadcasted_iota(jnp.int32, (query_rows, fresh_pad), 0), new)
    fresh_mask = lax.broadcasted_iota(jnp.int32, (query_rows, fresh_pad), 1) <= step_of

    gather_rows(3)
    send_slots(3, 1)

    scale = math.sqrt(DH)
    contract_last = (((1,), (1,)), ((), ()))

    def weigh(kv_head):
        query = queries_by_head[kv_head].astype(jnp.bfloat16)
        cache_k = arrived[kv_head].reshape(slots, DH)
        cache_scores = (
            lax.dot_general(query, cache_k, contract_last, preferred_element_type=jnp.float32)
            / scale
        )
        fresh_scores = (
            lax.dot_general(
                query, fresh_rows[kv_head], contract_last, preferred_element_type=jnp.float32
            )
            / scale
        )
        cache_scores = jnp.where(cache_mask, cache_scores, -1e30)
        fresh_scores = jnp.where(fresh_mask, fresh_scores, -1e30)
        highest = jnp.maximum(
            jnp.max(cache_scores, axis=-1, keepdims=True),
            jnp.max(fresh_scores, axis=-1, keepdims=True),
        )
        cache_weights = jnp.where(cache_mask, jnp.exp(cache_scores - highest), 0.0)
        fresh_weights = jnp.where(fresh_mask, jnp.exp(fresh_scores - highest), 0.0)
        weight_sum = jnp.sum(cache_weights, axis=-1, keepdims=True) + jnp.sum(
            fresh_weights, axis=-1, keepdims=True
        )
        return cache_weights.astype(jnp.bfloat16), fresh_weights.astype(jnp.bfloat16), weight_sum

    head_copies = {}

    def blend(kv_head, weights):
        cache_weights, fresh_weights, weight_sum = weights
        cache_v = arrived[per_weight + kv_head].reshape(slots, DH)
        blended = jnp.dot(cache_weights, cache_v, preferred_element_type=jnp.float32) + jnp.dot(
            fresh_weights, fresh_rows[per_weight + kv_head], preferred_element_type=jnp.float32
        )
        result = blended / weight_sum
        for member in range(group_size):
            heads[:, member * DH : (member + 1) * DH] = result[member * new : (member + 1) * new]
        heads_rounded[kv_head] = heads[...].astype(jnp.bfloat16)
        for relation in far_first:
            copy = remote(
                heads_rounded.at[kv_head],
                heads_all.at[kv_head, me],
                head_send.at[kv_head, relation],
                head_recv.at[kv_head, relation],
                tensor=peer(relation),
            )
            copy.start()
            head_copies[kv_head, relation] = copy
        heads_all[kv_head, me] = heads_rounded[kv_head]

    kv_out = group_size * DH

    def gathered_heads(kv_head):
        for relation in far_first[::-1]:
            head_copies[kv_head, relation].wait_recv()
        for source in range(peers):
            heads_flat[kv_head, source * new : (source + 1) * new, :] = heads_all[
                kv_head, source
            ].astype(jnp.float32)
        return heads_flat[kv_head].astype(jnp.bfloat16)

    wait_slots(0)
    weights_of = [weigh(kv_head) for kv_head in range(kv_heads)]
    wait_slots(2)
    blend(0, weights_of[0])
    wait_slots(3)
    blend(1, weights_of[1])

    load_out.wait()
    out_half = section_out.shape[2]
    flat = gathered_heads(0)
    for part in range(2):
        section_out[part] = jnp.dot(
            flat,
            out_weight[:kv_out, part * out_half : (part + 1) * out_half],
            preferred_element_type=jnp.float32,
        )
    flat = gathered_heads(1)
    section_copies = {}
    for part in range(2):
        section_out[part] = section_out[part] + jnp.dot(
            flat,
            out_weight[kv_out:, part * out_half : (part + 1) * out_half],
            preferred_element_type=jnp.float32,
        )
        copy = remote(
            section_out.at[part],
            section_in.at[part],
            sec_send.at[part],
            sec_recv.at[part],
            section=1 - core,
        )
        copy.start()
        section_copies[part] = copy
    for part in range(2):
        section_copies[part].wait_recv()
        out_ref[:, part * out_half : (part + 1) * out_half] = (
            section_out[part] + section_in[part]
        ).astype(jnp.bfloat16)

    for copies in (
        act_copies, twin_copies, fresh_copies, owner_copies, x_copies, z_copies, part_copies,
        slot_copies, head_copies, section_copies,
    ):
        for copy in copies.values():
            copy.wait_send()
    for copy in weight_copies:
        copy.wait_send()
    for _, copy in pass_copies:
        copy.wait_send()


def split_contraction(hidden_rows, fresh_rows, owners, key_weight, value_weight, queries, out_weight):
    peers = lax.axis_size("tensor")
    groups = lax.axis_size("groups")
    quad = peers // 2
    rows_here, width = hidden_rows.shape
    new = fresh_rows.shape[1]
    piece = width // peers
    kv_width = key_weight.shape[1]
    capacity = max(2, 2 * rows_here // peers)
    padded = rows_here + 16
    sent_rows = rows_here + 8
    query_width = queries.shape[2]
    kv_heads = kv_width // DH
    query_rows = new * query_width // (kv_heads * DH)
    out_width = out_weight.shape[1]
    bf16, f32 = jnp.bfloat16, jnp.float32
    dma = pltpu.SemaphoreType.DMA
    in_vmem = pl.BlockSpec(memory_space=pltpu.VMEM)
    in_hbm = pl.BlockSpec(memory_space=pltpu.HBM)
    chunks = 2 * kv_width // DH
    pieces = len(weight_pieces(chunks, piece // groups))
    flat = pl.pallas_call(
        functools.partial(rebuild_kernel, peers, groups),
        out_shape=jax.ShapeDtypeStruct((peers * new, out_width), bf16),
        in_specs=[in_hbm] * 7,
        out_specs=in_vmem,
        scratch_shapes=[
            pltpu.VMEM(fresh_rows.shape, bf16),
            pltpu.VMEM((1, rows_here), jnp.int32),
            pltpu.VMEM(key_weight.shape, bf16),
            pltpu.VMEM(value_weight.shape, bf16),
            pltpu.VMEM(queries.shape, bf16),
            pltpu.VMEM((rows_here // 2, width), bf16),
            pltpu.VMEM((quad, 2, rows_here // 2, piece), bf16),
            pltpu.VMEM((quad, 2, new, piece), bf16),
            pltpu.VMEM((2, quad, padded, piece), bf16),
            pltpu.VMEM((quad, 2, new, piece), bf16),
            pltpu.VMEM((chunks, piece, DH), bf16),
            pltpu.VMEM((chunks, quad, padded, DH), f32),
            pltpu.VMEM((chunks, 2, sent_rows, DH), f32),
            pltpu.VMEM((chunks, sent_rows, DH), f32),
            pltpu.VMEM((chunks, quad - 1, sent_rows, DH), f32),
            pltpu.VMEM((chunks, peers, capacity, DH), bf16),
            pltpu.VMEM((chunks, peers, capacity, DH), bf16),
            pltpu.VMEM((peers, 1, rows_here), jnp.int32),
            pltpu.VMEM((kv_heads, query_rows, DH), f32),
            pltpu.VMEM((new, query_width // kv_heads), f32),
            pltpu.VMEM((kv_heads, new, query_width // kv_heads), bf16),
            pltpu.VMEM((kv_heads, peers, new, query_width // kv_heads), bf16),
            pltpu.VMEM((kv_heads, peers * new, query_width // kv_heads), f32),
            pltpu.VMEM(out_weight.shape, bf16),
            pltpu.VMEM((2, peers * new, out_width // 2), f32),
            pltpu.VMEM((2, peers * new, out_width // 2), f32),
            dma((7,)),
            dma((pieces,)),
            dma((pieces,)),
            dma((pieces,)),
            dma((pieces,)),
            dma((quad,)),
            dma((quad,)),
            dma((quad,)),
            dma((quad,)),
            dma((quad,)),
            dma((quad,)),
            dma((chunks,)),
            dma((chunks,)),
            dma((chunks,)),
            dma((chunks,)),
            dma((chunks, quad)),
            dma((chunks, quad)),
            dma((peers,)),
            dma((peers,)),
            dma((chunks, peers)),
            dma((chunks, peers)),
            dma((kv_heads, peers)),
            dma((kv_heads, peers)),
            dma((2,)),
            dma((2,)),
            pltpu.SemaphoreType.REGULAR,
        ],
        compiler_params=pltpu.CompilerParams(
            collective_id=0, has_side_effects=True, vmem_limit_bytes=60 * 1024 * 1024
        ),
    )(
        hidden_rows,
        fresh_rows,
        owners.reshape(1, rows_here),
        key_weight,
        value_weight,
        queries,
        out_weight,
    )
    return flat.reshape(peers, new, out_width)


def per_device(hidden_rows, *others):
    peers = lax.axis_size("tensor")
    rows_here, width = hidden_rows.shape
    fits = (
        lax.axis_size("groups") == 2
        and lax.axis_size("section") == 2
        and peers == 8
        and width % (peers * 256) == 0
        and rows_here % 128 == 0
        and others[-1].shape[1] % 256 == 0
        and (2 * rows_here) % (peers * 16) == 0
    )
    if fits:
        return split_contraction(hidden_rows, *others)
    return gathered_weights(hidden_rows, *others)


def solution(mesh):
    return jax.shard_map(
        per_device,
        mesh=mesh,
        in_specs=(
            P(("groups", "tensor"), None),
            P(("groups", "tensor"), None, None),
            P(("groups", "tensor"), None),
            P("tensor", "section"),
            P("tensor", "section"),
            P(("groups", "tensor"), None, "section"),
            P("section", "tensor"),
        ),
        out_specs=P("groups", None, "tensor"),
        check_vma=False,
    )
```

```python
import functools
import math

import jax
import jax.numpy as jnp
from jax import lax
from jax.experimental import pallas as pl
from jax.experimental.pallas import tpu as pltpu
from jax.sharding import PartitionSpec as P

DH = 128


norm_eps = 1e-05


def rms_rows(row_block):
    widened = row_block.astype(jnp.float32)
    factor = lax.rsqrt(jnp.mean(widened * widened, axis=-1, keepdims=True) + norm_eps)
    return (widened * factor).astype(jnp.bfloat16)


def attend(query_rows, cache_keys, cache_values, cache_valid, fresh_keys, fresh_values):
    steps_new = query_rows.shape[0]
    kv_heads = cache_keys.shape[1] // DH
    group_size = query_rows.shape[1] // (kv_heads * DH)
    query_heads = query_rows.reshape(steps_new, kv_heads, group_size, DH)
    cache_k = cache_keys.reshape(-1, kv_heads, DH)
    cache_v = cache_values.reshape(-1, kv_heads, DH)
    fresh_k = fresh_keys.reshape(-1, kv_heads, DH)
    fresh_v = fresh_values.reshape(-1, kv_heads, DH)
    cache_scores = jnp.einsum(
        "tkgd,skd->tkgs", query_heads, cache_k, preferred_element_type=jnp.float32
    ) / math.sqrt(DH)
    fresh_scores = jnp.einsum(
        "tkgd,skd->tkgs", query_heads, fresh_k, preferred_element_type=jnp.float32
    ) / math.sqrt(DH)
    visible = jnp.arange(steps_new)[None, :] <= jnp.arange(steps_new)[:, None]
    cache_mask = cache_valid[None, None, None, :]
    fresh_mask = visible[:, None, None, :]
    cache_scores = jnp.where(cache_mask, cache_scores, -1e30)
    fresh_scores = jnp.where(fresh_mask, fresh_scores, -1e30)
    highest = jnp.maximum(jnp.max(cache_scores, axis=-1), jnp.max(fresh_scores, axis=-1))[..., None]
    cache_weights = jnp.where(cache_mask, jnp.exp(cache_scores - highest), 0.0)
    fresh_weights = jnp.where(fresh_mask, jnp.exp(fresh_scores - highest), 0.0)
    weight_sum = jnp.sum(cache_weights, axis=-1) + jnp.sum(fresh_weights, axis=-1)
    blended = jnp.einsum(
        "tkgs,skd->tkgd",
        cache_weights.astype(jnp.bfloat16),
        cache_v,
        preferred_element_type=jnp.float32,
    )
    blended = blended + jnp.einsum(
        "tkgs,skd->tkgd",
        fresh_weights.astype(jnp.bfloat16),
        fresh_v,
        preferred_element_type=jnp.float32,
    )
    result_heads = blended / weight_sum[..., None]
    return result_heads.reshape(steps_new, -1).astype(jnp.bfloat16)


def project_rows(normed, key_weight, value_weight):
    key_sums = jnp.dot(
        normed,
        lax.all_gather(key_weight, "tensor", axis=0, tiled=True),
        preferred_element_type=jnp.float32,
    )
    value_sums = jnp.dot(
        normed,
        lax.all_gather(value_weight, "tensor", axis=0, tiled=True),
        preferred_element_type=jnp.float32,
    )
    return (key_sums.astype(jnp.bfloat16), value_sums.astype(jnp.bfloat16))


def slot_layout(owners, peers, capacity):
    target = owners[:, 0]
    onehot = (target[:, None] == jnp.arange(peers, dtype=jnp.int32)[None, :]).astype(jnp.int32)
    rows = jnp.arange(target.shape[0], dtype=jnp.int32)
    earlier = (target[:, None] == target[None, :]) & (rows[None, :] < rows[:, None])
    within = jnp.sum(earlier.astype(jnp.int32), axis=1)
    counts = jnp.sum(onehot, axis=0)
    return (target * capacity + within, counts)


def fill_slots(payload, slot_index, peers, capacity):
    buffer = (
        jnp.zeros((peers * capacity, payload.shape[1]), payload.dtype).at[slot_index].set(payload)
    )
    return buffer.reshape(peers, capacity, payload.shape[1])


def gathered_weights(hidden_rows, fresh_rows, owners, key_weight, value_weight, queries, out_weight):
    peers = lax.axis_size("tensor")
    rows_here = hidden_rows.shape[0]
    capacity = max(2, 2 * rows_here // peers)
    slot_index, counts = slot_layout(owners, peers, capacity)
    slot_total = peers * capacity
    normed = rms_rows(jnp.concatenate([hidden_rows, fresh_rows[0]], axis=0))
    key_rows, value_rows = project_rows(normed, key_weight, value_weight)
    local_pairs = jnp.concatenate([key_rows[:rows_here], value_rows[:rows_here]], axis=1)
    outgoing = fill_slots(local_pairs, slot_index, peers, capacity)
    arrived, arrived_counts = (
        lax.all_to_all(outgoing, "tensor", split_axis=0, concat_axis=0, tiled=True),
        lax.all_to_all(counts.reshape(peers, 1), "tensor", split_axis=0, concat_axis=0, tiled=True),
    )
    flat_pairs = arrived.reshape(slot_total, -1)
    half_width = key_rows.shape[1]
    cache_keys, cache_values = (flat_pairs[:, :half_width], flat_pairs[:, half_width:])
    fresh_keys, fresh_values = (key_rows[rows_here:], value_rows[rows_here:])
    cache_valid = (jnp.arange(capacity, dtype=jnp.int32)[None, :] < arrived_counts).reshape(-1)
    head_block = attend(queries[0], cache_keys, cache_values, cache_valid, fresh_keys, fresh_values)
    piece = lax.all_gather(head_block[None], "tensor", axis=0, tiled=True)
    flat_piece = piece.reshape(-1, piece.shape[-1])
    partial_rows = jnp.dot(flat_piece, out_weight, preferred_element_type=jnp.float32)
    partial_out = partial_rows.reshape(piece.shape[0], piece.shape[1], -1)
    summed = lax.psum(partial_out, "section")
    return summed.astype(jnp.bfloat16)


def row_factor(widened_squares, width):
    return lax.rsqrt(widened_squares / width + norm_eps)


def weight_pieces(chunks, share):
    pieces = []
    for chunk in range(chunks):
        cuts = 2 if chunk == chunks - 1 else 1
        rows = share // cuts
        pieces.extend((chunk, cut * rows, rows) for cut in range(cuts))
    return pieces


def rebuild_kernel(
    peers,
    groups,
    hidden_hbm,
    fresh_hbm,
    owner_hbm,
    key_hbm,
    value_hbm,
    query_hbm,
    out_weight_hbm,
    out_ref,
    fresh_ref,
    owner_row,
    key_ref,
    value_ref,
    query_ref,
    own_rows,
    normed,
    fresh_normed,
    lhs,
    fresh_in,
    far_weights,
    parts,
    parts_x,
    parts_z,
    parts_in,
    outgoing,
    arrived,
    owner_all,
    queries_by_head,
    heads,
    heads_rounded,
    heads_all,
    heads_flat,
    out_weight,
    section_out,
    section_in,
    local_sem,
    weight_send,
    weight_recv,
    pass_send,
    pass_recv,
    act_send,
    act_recv,
    twin_send,
    twin_recv,
    fresh_send,
    fresh_recv,
    x_send,
    x_recv,
    z_send,
    z_recv,
    part_send,
    part_recv,
    owner_send,
    owner_recv,
    slot_send,
    slot_recv,
    head_send,
    head_recv,
    sec_send,
    sec_recv,
    met_sem,
):
    quad = peers // 2
    me = lax.axis_index("tensor")
    core = lax.axis_index("section")
    group = lax.axis_index("groups")
    q = lax.rem(me, quad)
    half = me // quad
    x_of = lax.rem(me, 2)
    z_of = q // 2

    def peer(relation):
        z = 1 - z_of if relation & 1 else z_of
        x = 1 - x_of if relation & 2 else x_of
        h = 1 - half if relation & 4 else half
        return h * quad + z * 2 + x

    def piece_of(relation):
        return peer(relation & 3) - half * quad

    rows_half = own_rows.shape[0]
    rows_here = 2 * rows_half
    width = own_rows.shape[1]
    piece = width // peers
    kv_width = key_ref.shape[1]
    share = piece // groups
    padded = lhs.shape[2]
    sent_rows = parts_in.shape[2]

    def remote(source, target, send, recv, **where):
        return pltpu.make_async_remote_copy(
            src_ref=source,
            dst_ref=target,
            send_sem=send,
            recv_sem=recv,
            device_id=where,
            device_id_type=pl.DeviceIdType.MESH,
        )

    rows_mine = pl.ds(pl.multiple_of(core * rows_half, rows_half), rows_half)
    load_rows = pltpu.make_async_copy(hidden_hbm.at[rows_mine, :], own_rows, local_sem.at[0])
    load_rows.start()
    load_owner = pltpu.make_async_copy(owner_hbm, owner_row, local_sem.at[1])
    load_fresh = pltpu.make_async_copy(fresh_hbm, fresh_ref, local_sem.at[2])
    load_key = pltpu.make_async_copy(key_hbm, key_ref, local_sem.at[3])
    load_value = pltpu.make_async_copy(value_hbm, value_ref, local_sem.at[4])
    load_query = pltpu.make_async_copy(query_hbm, query_ref, local_sem.at[5])
    load_out = pltpu.make_async_copy(out_weight_hbm, out_weight, local_sem.at[6])
    load_owner.start()
    load_fresh.start()
    load_key.start()
    load_value.start()

    far_first = (7, 5, 6, 4, 3, 1, 2)
    barrier = pltpu.get_barrier_semaphore()
    for relation in (5, 3, 1, 2):
        pl.semaphore_signal(
            barrier, inc=1, device_id={"tensor": peer(relation)},
            device_id_type=pl.DeviceIdType.MESH,
        )
    pl.semaphore_signal(
        barrier, inc=1, device_id={"groups": 1 - group}, device_id_type=pl.DeviceIdType.MESH
    )
    pl.semaphore_signal(
        barrier, inc=1, device_id={"section": 1 - core}, device_id_type=pl.DeviceIdType.MESH
    )

    chunks = 2 * kv_width // DH
    per_weight = kv_width // DH
    pieces = weight_pieces(chunks, share)
    weight_copies = []
    pass_refs = []
    for index, (chunk, first_row, rows) in enumerate(pieces):
        weight = (key_hbm, value_hbm)[chunk // per_weight]
        first = (chunk % per_weight) * DH
        span = pl.ds(pl.multiple_of(group * share + first_row, 16), rows)
        weight_copies.append(
            remote(
                weight.at[span, first : first + DH],
                far_weights.at[chunk, span, :],
                weight_send.at[index],
                weight_recv.at[index],
                tensor=peer(5),
            )
        )
        pass_refs.append(far_weights.at[chunk, span, :])

    load_rows.wait()
    squares = jnp.zeros((rows_half, 1), jnp.float32)
    for slice_index in range(peers):
        block = own_rows[:, slice_index * piece : (slice_index + 1) * piece].astype(jnp.float32)
        squares = squares + jnp.sum(block * block, axis=-1, keepdims=True)
    factor = row_factor(squares, width)
    for slice_index in range(peers):
        side = lax.rem(slice_index // quad + half, 2)
        block = own_rows[:, slice_index * piece : (slice_index + 1) * piece].astype(jnp.float32)
        normed[lax.rem(slice_index + 2 * side, quad), side] = (block * factor).astype(jnp.bfloat16)
    load_fresh.wait()
    fresh = fresh_ref[0].astype(jnp.float32)
    fresh_factor = row_factor(jnp.sum(fresh * fresh, axis=-1, keepdims=True), width)
    for slice_index in range(peers):
        side = lax.rem(slice_index // quad + half, 2)
        block = fresh[:, slice_index * piece : (slice_index + 1) * piece]
        fresh_normed[lax.rem(slice_index + 2 * side, quad), side] = (block * fresh_factor).astype(
            jnp.bfloat16
        )
    pl.semaphore_wait(barrier, 6)

    act_copies = {}
    twin_copies = {}

    def to_twin(source, relation):
        copy = remote(
            source,
            lhs.at[:, relation, rows_mine, :],
            twin_send.at[relation],
            twin_recv.at[relation],
            section=1 - core,
        )
        copy.start()
        twin_copies[relation] = copy

    for relation in (3, 1, 2):
        copy = remote(
            normed.at[piece_of(relation)],
            lhs.at[:, relation, rows_mine, :],
            act_send.at[relation],
            act_recv.at[relation],
            tensor=peer(relation),
        )
        copy.start()
        act_copies[relation] = copy
    to_twin(normed.at[q], 0)
    fresh_copies = {}
    for relation in (3, 1, 2):
        copy = remote(
            fresh_normed.at[piece_of(relation)],
            fresh_in.at[relation],
            fresh_send.at[relation],
            fresh_recv.at[relation],
            tensor=peer(relation),
        )
        copy.start()
        fresh_copies[relation] = copy
    fresh_in[0] = fresh_normed[q]

    ahead = 99
    for copy in weight_copies[:ahead]:
        copy.start()
    pl.semaphore_signal(
        met_sem, inc=1, device_id={"tensor": peer(5)}, device_id_type=pl.DeviceIdType.MESH
    )
    load_query.start()
    load_out.start()
    lhs[:, 0, rows_mine, :] = normed[q]

    load_owner.wait()
    pl.semaphore_wait(met_sem, 1)
    owner_copies = {}
    for relation in far_first:
        copy = remote(
            owner_row,
            owner_all.at[me],
            owner_send.at[relation],
            owner_recv.at[relation],
            tensor=peer(relation),
        )
        copy.start()
        owner_copies[relation] = copy
    owner_all[me] = owner_row[...]

    new = fresh.shape[0]
    capacity = arrived.shape[2]
    slots = peers * capacity
    rows_of = owner_row[...]
    earlier = lax.broadcasted_iota(jnp.int32, (rows_here, rows_here), 0) < lax.broadcasted_iota(
        jnp.int32, (rows_here, rows_here), 1
    )
    rows_float = jnp.broadcast_to(rows_of.astype(jnp.float32), (rows_here, rows_here))
    same = jnp.logical_and(rows_float.T == rows_float, earlier)
    within = jnp.sum(jnp.where(same, 1.0, 0.0), axis=0, keepdims=True).astype(jnp.int32)
    slot_of = rows_of * capacity + within
    slot_pick = jnp.where(
        lax.broadcasted_iota(jnp.int32, (slots, rows_here), 0) == slot_of, 1.0, 0.0
    ).astype(jnp.bfloat16)

    load_query.wait()
    kv_heads = kv_width // DH
    group_size = query_ref.shape[2] // (kv_heads * DH)
    for head in range(kv_heads * group_size):
        queries_by_head[head // group_size, pl.ds((head % group_size) * new, new), :] = query_ref[
            0, :, head * DH : (head + 1) * DH
        ].astype(jnp.float32)

    load_key.wait()
    load_value.wait()

    def add_block(relation):
        for side in range(2):
            lhs[side, relation, rows_here:, :] = jnp.zeros(
                (padded - rows_here, piece), jnp.bfloat16
            )
            lhs[side, relation, rows_here : rows_here + new, :] = fresh_in[relation, side]
        near = lhs[0, relation]
        for which, weight in enumerate((key_ref, value_ref)):
            product = jnp.dot(near, weight[...], preferred_element_type=jnp.float32)
            for column in range(per_weight):
                parts[which * per_weight + column, relation] = product[
                    :, column * DH : (column + 1) * DH
                ]

    pass_copies = []

    def pass_on(chunk):
        for index, (of_chunk, _, _) in enumerate(pieces):
            if of_chunk != chunk:
                continue
            weight_copies[index].wait_recv()
            copy = remote(
                pass_refs[index],
                pass_refs[index],
                pass_send.at[index],
                pass_recv.at[index],
                groups=1 - group,
            )
            copy.start()
            pass_copies.append((chunk, copy))

    part_copies = {}
    x_copies = {}
    z_copies = {}
    slot_copies = {}
    fresh_rows = {}
    fresh_pad = padded - rows_here

    def multiply_far(chunk):
        for of_chunk, copy in pass_copies:
            if of_chunk == chunk:
                copy.wait_recv()
        product = jnp.dot(
            lhs[1].reshape(quad * padded, piece),
            far_weights[chunk],
            preferred_element_type=jnp.float32,
        )
        parts[chunk] = parts[chunk] + product.reshape(quad, padded, DH)

    def send_x(chunk):
        copy = remote(
            parts.at[chunk, pl.ds(2, 2), pl.ds(0, sent_rows), :],
            parts_x.at[chunk],
            x_send.at[chunk],
            x_recv.at[chunk],
            tensor=peer(2),
        )
        copy.start()
        x_copies[chunk] = copy

    def send_z(chunk):
        x_copies[chunk].wait_recv()
        parts[chunk, 1, :sent_rows] = parts[chunk, 1, :sent_rows] + parts_x[chunk, 1]
        copy = remote(
            parts.at[chunk, 1, pl.ds(0, sent_rows), :],
            parts_z.at[chunk],
            z_send.at[chunk],
            z_recv.at[chunk],
            tensor=peer(1),
        )
        copy.start()
        z_copies[chunk] = copy

    def send_direct(chunk):
        for relation in (2, 3, 1):
            copy = remote(
                parts.at[chunk, relation, pl.ds(0, sent_rows), :],
                parts_in.at[chunk, relation - 1],
                part_send.at[chunk, relation],
                part_recv.at[chunk, relation],
                tensor=peer(relation),
            )
            copy.start()
            part_copies[chunk, relation] = copy

    def gather_rows(chunk):
        total = parts[chunk, 0, :sent_rows]
        if chunk in x_copies:
            z_copies[chunk].wait_recv()
            total = total + parts_x[chunk, 0] + parts_z[chunk]
        else:
            for relation in (2, 1, 3):
                part_copies[chunk, relation].wait_recv()
                total = total + parts_in[chunk, relation - 1]
        placed = jnp.dot(
            slot_pick,
            total[:rows_here].astype(jnp.bfloat16),
            preferred_element_type=jnp.float32,
        ).astype(jnp.bfloat16)
        outgoing[chunk] = placed.reshape(peers, capacity, DH)
        fresh_rows[chunk] = jnp.concatenate(
            [
                total[rows_here:],
                jnp.zeros((fresh_pad - (sent_rows - rows_here), DH), jnp.float32),
            ],
            axis=0,
        ).astype(jnp.bfloat16)

    def send_slots(first, count):
        span = pl.ds(first, count)
        for relation in far_first:
            copy = remote(
                outgoing.at[span, peer(relation)],
                arrived.at[span, me],
                slot_send.at[first, relation],
                slot_recv.at[first, relation],
                tensor=peer(relation),
            )
            copy.start()
            slot_copies[first, relation] = copy
        arrived[span, me] = outgoing[span, me]

    def wait_slots(first):
        for relation in far_first[::-1]:
            slot_copies[first, relation].wait_recv()

    twin_copies[0].wait_recv()
    add_block(0)
    for relation in (3, 1, 2):
        act_copies[relation].wait_recv()
        to_twin(lhs.at[:, relation, rows_mine, :], relation)
    for relation in (3, 1, 2):
        twin_copies[relation].wait_recv()
        fresh_copies[relation].wait_recv()
        add_block(relation)
    pass_on(0)
    pass_on(1)
    multiply_far(0)
    send_direct(0)
    pass_on(2)
    multiply_far(1)
    send_direct(1)
    pass_on(3)
    multiply_far(2)
    send_direct(2)
    multiply_far(3)
    send_direct(3)
    gather_rows(0)
    gather_rows(1)
    gather_rows(2)
    send_slots(2, 1)
    send_slots(0, per_weight)
    for relation in far_first:
        owner_copies[relation].wait_recv()
    slot_mask = []
    for source in range(peers):
        count = jnp.sum(jnp.where(owner_all[source] == me, 1.0, 0.0), axis=-1, keepdims=True)
        place = lax.broadcasted_iota(jnp.int32, (capacity, DH), 0).astype(jnp.float32)
        slot_mask.append(jnp.where(place < count, 1.0, 0.0))
    slot_mask = jnp.concatenate(slot_mask, axis=0).T
    query_rows = new * group_size
    cache_mask = slot_mask[:query_rows] > 0.5
    step_of = lax.rem(lax.broadcasted_iota(jnp.int32, (query_rows, fresh_pad), 0), new)
    fresh_mask = lax.broadcasted_iota(jnp.int32, (query_rows, fresh_pad), 1) <= step_of

    gather_rows(3)
    send_slots(3, 1)

    scale = math.sqrt(DH)
    contract_last = (((1,), (1,)), ((), ()))

    def weigh(kv_head):
        query = queries_by_head[kv_head].astype(jnp.bfloat16)
        cache_k = arrived[kv_head].reshape(slots, DH)
        cache_scores = (
            lax.dot_general(query, cache_k, contract_last, preferred_element_type=jnp.float32)
            / scale
        )
        fresh_scores = (
            lax.dot_general(
                query, fresh_rows[kv_head], contract_last, preferred_element_type=jnp.float32
            )
            / scale
        )
        cache_scores = jnp.where(cache_mask, cache_scores, -1e30)
        fresh_scores = jnp.where(fresh_mask, fresh_scores, -1e30)
        highest = jnp.maximum(
            jnp.max(cache_scores, axis=-1, keepdims=True),
            jnp.max(fresh_scores, axis=-1, keepdims=True),
        )
        cache_weights = jnp.where(cache_mask, jnp.exp(cache_scores - highest), 0.0)
        fresh_weights = jnp.where(fresh_mask, jnp.exp(fresh_scores - highest), 0.0)
        weight_sum = jnp.sum(cache_weights, axis=-1, keepdims=True) + jnp.sum(
            fresh_weights, axis=-1, keepdims=True
        )
        return cache_weights.astype(jnp.bfloat16), fresh_weights.astype(jnp.bfloat16), weight_sum

    head_copies = {}

    def blend(kv_head, weights):
        cache_weights, fresh_weights, weight_sum = weights
        cache_v = arrived[per_weight + kv_head].reshape(slots, DH)
        blended = jnp.dot(cache_weights, cache_v, preferred_element_type=jnp.float32) + jnp.dot(
            fresh_weights, fresh_rows[per_weight + kv_head], preferred_element_type=jnp.float32
        )
        result = blended / weight_sum
        for member in range(group_size):
            heads[:, member * DH : (member + 1) * DH] = result[member * new : (member + 1) * new]
        heads_rounded[kv_head] = heads[...].astype(jnp.bfloat16)
        for relation in far_first:
            copy = remote(
                heads_rounded.at[kv_head],
                heads_all.at[kv_head, me],
                head_send.at[kv_head, relation],
                head_recv.at[kv_head, relation],
                tensor=peer(relation),
            )
            copy.start()
            head_copies[kv_head, relation] = copy
        heads_all[kv_head, me] = heads_rounded[kv_head]

    kv_out = group_size * DH

    def gathered_heads(kv_head):
        for relation in far_first[::-1]:
            head_copies[kv_head, relation].wait_recv()
        for source in range(peers):
            heads_flat[kv_head, source * new : (source + 1) * new, :] = heads_all[
                kv_head, source
            ].astype(jnp.float32)
        return heads_flat[kv_head].astype(jnp.bfloat16)

    wait_slots(0)
    weights_of = [weigh(kv_head) for kv_head in range(kv_heads)]
    wait_slots(2)
    blend(0, weights_of[0])
    wait_slots(3)
    blend(1, weights_of[1])

    load_out.wait()
    out_half = section_out.shape[2]
    flat = gathered_heads(0)
    for part in range(2):
        section_out[part] = jnp.dot(
            flat,
            out_weight[:kv_out, part * out_half : (part + 1) * out_half],
            preferred_element_type=jnp.float32,
        )
    flat = gathered_heads(1)
    section_copies = {}
    for part in range(2):
        section_out[part] = section_out[part] + jnp.dot(
            flat,
            out_weight[kv_out:, part * out_half : (part + 1) * out_half],
            preferred_element_type=jnp.float32,
        )
        copy = remote(
            section_out.at[part],
            section_in.at[part],
            sec_send.at[part],
            sec_recv.at[part],
            section=1 - core,
        )
        copy.start()
        section_copies[part] = copy
    for part in range(2):
        section_copies[part].wait_recv()
        out_ref[:, part * out_half : (part + 1) * out_half] = (
            section_out[part] + section_in[part]
        ).astype(jnp.bfloat16)

    for copies in (
        act_copies, twin_copies, fresh_copies, owner_copies, x_copies, z_copies, part_copies,
        slot_copies, head_copies, section_copies,
    ):
        for copy in copies.values():
            copy.wait_send()
    for copy in weight_copies:
        copy.wait_send()
    for _, copy in pass_copies:
        copy.wait_send()


def split_contraction(hidden_rows, fresh_rows, owners, key_weight, value_weight, queries, out_weight):
    peers = lax.axis_size("tensor")
    groups = lax.axis_size("groups")
    quad = peers // 2
    rows_here, width = hidden_rows.shape
    new = fresh_rows.shape[1]
    piece = width // peers
    kv_width = key_weight.shape[1]
    capacity = max(2, 2 * rows_here // peers)
    padded = rows_here + 16
    sent_rows = rows_here + 8
    query_width = queries.shape[2]
    kv_heads = kv_width // DH
    query_rows = new * query_width // (kv_heads * DH)
    out_width = out_weight.shape[1]
    bf16, f32 = jnp.bfloat16, jnp.float32
    dma = pltpu.SemaphoreType.DMA
    in_vmem = pl.BlockSpec(memory_space=pltpu.VMEM)
    in_hbm = pl.BlockSpec(memory_space=pltpu.HBM)
    chunks = 2 * kv_width // DH
    pieces = len(weight_pieces(chunks, piece // groups))
    flat = pl.pallas_call(
        functools.partial(rebuild_kernel, peers, groups),
        out_shape=jax.ShapeDtypeStruct((peers * new, out_width), bf16),
        in_specs=[in_hbm] * 7,
        out_specs=in_vmem,
        scratch_shapes=[
            pltpu.VMEM(fresh_rows.shape, bf16),
            pltpu.VMEM((1, rows_here), jnp.int32),
            pltpu.VMEM(key_weight.shape, bf16),
            pltpu.VMEM(value_weight.shape, bf16),
            pltpu.VMEM(queries.shape, bf16),
            pltpu.VMEM((rows_here // 2, width), bf16),
            pltpu.VMEM((quad, 2, rows_here // 2, piece), bf16),
            pltpu.VMEM((quad, 2, new, piece), bf16),
            pltpu.VMEM((2, quad, padded, piece), bf16),
            pltpu.VMEM((quad, 2, new, piece), bf16),
            pltpu.VMEM((chunks, piece, DH), bf16),
            pltpu.VMEM((chunks, quad, padded, DH), f32),
            pltpu.VMEM((chunks, 2, sent_rows, DH), f32),
            pltpu.VMEM((chunks, sent_rows, DH), f32),
            pltpu.VMEM((chunks, quad - 1, sent_rows, DH), f32),
            pltpu.VMEM((chunks, peers, capacity, DH), bf16),
            pltpu.VMEM((chunks, peers, capacity, DH), bf16),
            pltpu.VMEM((peers, 1, rows_here), jnp.int32),
            pltpu.VMEM((kv_heads, query_rows, DH), f32),
            pltpu.VMEM((new, query_width // kv_heads), f32),
            pltpu.VMEM((kv_heads, new, query_width // kv_heads), bf16),
            pltpu.VMEM((kv_heads, peers, new, query_width // kv_heads), bf16),
            pltpu.VMEM((kv_heads, peers * new, query_width // kv_heads), f32),
            pltpu.VMEM(out_weight.shape, bf16),
            pltpu.VMEM((2, peers * new, out_width // 2), f32),
            pltpu.VMEM((2, peers * new, out_width // 2), f32),
            dma((7,)),
            dma((pieces,)),
            dma((pieces,)),
            dma((pieces,)),
            dma((pieces,)),
            dma((quad,)),
            dma((quad,)),
            dma((quad,)),
            dma((quad,)),
            dma((quad,)),
            dma((quad,)),
            dma((chunks,)),
            dma((chunks,)),
            dma((chunks,)),
            dma((chunks,)),
            dma((chunks, quad)),
            dma((chunks, quad)),
            dma((peers,)),
            dma((peers,)),
            dma((chunks, peers)),
            dma((chunks, peers)),
            dma((kv_heads, peers)),
            dma((kv_heads, peers)),
            dma((2,)),
            dma((2,)),
            pltpu.SemaphoreType.REGULAR,
        ],
        compiler_params=pltpu.CompilerParams(
            collective_id=0, has_side_effects=True, vmem_limit_bytes=60 * 1024 * 1024
        ),
    )(
        hidden_rows,
        fresh_rows,
        owners.reshape(1, rows_here),
        key_weight,
        value_weight,
        queries,
        out_weight,
    )
    return flat.reshape(peers, new, out_width)


def per_device(hidden_rows, *others):
    peers = lax.axis_size("tensor")
    rows_here, width = hidden_rows.shape
    fits = (
        lax.axis_size("groups") == 2
        and lax.axis_size("section") == 2
        and peers == 8
        and width % (peers * 256) == 0
        and rows_here % 128 == 0
        and others[-1].shape[1] % 256 == 0
        and (2 * rows_here) % (peers * 16) == 0
    )
    if fits:
        return split_contraction(hidden_rows, *others)
    return gathered_weights(hidden_rows, *others)


def solution(mesh):
    return jax.shard_map(
        per_device,
        mesh=mesh,
        in_specs=(
            P(("groups", "tensor"), None),
            P(("groups", "tensor"), None, None),
            P(("groups", "tensor"), None),
            P("tensor", "section"),
            P("tensor", "section"),
            P(("groups", "tensor"), None, "section"),
            P("section", "tensor"),
        ),
        out_specs=P("groups", None, "tensor"),
        check_vma=False,
    )
```
